512 devices in a mesh: lev: 16 (over z_lo, y), lon: 32 (over x, z_hi, core).
Axes of the slice: x: 4, y: 8, z: 8 (z_hi: 4, z_lo: 2; z = z_hi * 2 + z_lo), core: 2. Of those that a mesh axis runs over, the one named last changes fastest.
Arguments:
- snapshot: bfloat16 [384, 48, 4096], P('lev', None, 'lon'), may hold values from -6 to 6
- cotangent: bfloat16 [384, 48, 4096], P(None, 'lev', 'lon'), may hold values from -6 to 6
- ocean_mask: int32 [48, 4096], P('lev', 'lon'), may hold values 0 or 1
- kernel: bfloat16 [384, 49], replicated, may hold values from -0.875 to 0.875
- norm_gain: float32 [384], replicated, may hold values from 0.1 to 1.9
- norm_shift: float32 [384], replicated, may hold values from -3 to 3
- weight_in: bfloat16 [384, 1536], replicated, may hold values from -0.3125 to 0.3125
- weight_out: bfloat16 [1536, 384], replicated, may hold values from -0.15625 to 0.15625
Outputs:
- result: bfloat16 [384, 48, 4096], P(None, 'lev', 'lon')
- d_snapshot: bfloat16 [384, 48, 4096], P('lev', None, 'lon')
- kernel_grad: float32 [384, 49], replicated
The draws below stay inside these ranges and needn't reach their ends.
All inputs are finite; a program needn't handle non-finite values. No bound on the sum of `ocean_mask` on one device may be relied on, other than what follows from the above.
Results may differ from the reference program's by a relative error of at most 0.0057.
Values may be sent and summed in bfloat16 or wider, within the bound.
A program may use at most 64 MiB of HBM per device.

```python
import jax
import jax.numpy as jnp
from jax import lax

C = 384
FF = 1536
TAPS = 7
LAT_DEV = 3
LAT_ALL = 48
LON_ALL = 4096


def set_ends(values, own_key, smallest, top_value):
    shape = values.shape
    place = [jax.random.randint(jax.random.fold_in(own_key, axis), (), 0, shape[axis]) for axis in range(len(shape))]
    values = values.at[tuple(place)].set(smallest)
    longest = shape.index(max(shape))
    place[longest] = (place[longest] + 1) % shape[longest]
    return values.at[tuple(place)].set(top_value)


def levels(key, shape, shards, smallest, top_value):
    loudness, own = 1.0, jax.random.fold_in(key, 6)
    for dim, shards_of in shards:
        steps = jnp.exp(jax.random.uniform(jax.random.fold_in(own, dim), (shards_of,), jnp.float32, smallest / len(shards), top_value / len(shards)))
        loudness = loudness * jnp.repeat(steps, shape[dim] // shards_of).reshape([-1 if axis == dim else 1 for axis in range(len(shape))])
    return loudness


def noise(rng, dims, scale, most, cuts=(), kind=jnp.bfloat16):
    factor_of = levels(rng, dims, cuts, -0.22, 0.18) if cuts else 1.0
    values = jax.random.normal(rng, dims, jnp.float32) * scale * factor_of
    return jnp.minimum(jnp.maximum(values, -most), most).astype(kind)


def setup_inputs(seed: int = 0) -> dict:
    key_of = jax.random.split(jax.random.key(seed), 9)
    return {
        "snapshot": noise(key_of[0], (C, LAT_ALL, LON_ALL), 1.0, 6.0, ((0, 16), (2, 32))),
        "cotangent": noise(key_of[1], (C, LAT_ALL, LON_ALL), 1.0, 6.0, ((1, 16), (2, 32))),
        "ocean_mask": set_ends((jax.random.randint(key_of[2], (LAT_ALL, LON_ALL), 0, 4) < 3).astype(jnp.int32), jax.random.fold_in(key_of[2], 1), 0, 1),
        "kernel": noise(key_of[3], (C, TAPS * TAPS), (TAPS * TAPS) ** -0.5, 0.875),
        "norm_gain": jnp.clip(1.0 + 0.18 * jax.random.normal(key_of[4], (C,), jnp.float32), 0.1, 1.9),
        "norm_shift": noise(key_of[5], (C,), 0.5, 3.0, (), jnp.float32),
        "weight_in": noise(key_of[6], (C, FF), C ** -0.5, 0.3125),
        "weight_out": noise(key_of[7], (FF, C), FF ** -0.5, 0.15625),
    }


epsilon = 1e-06
root_half = 0.7071067811865476
inv_root_tau = 0.3989422804014327

def fold_pad(values):
    reach = TAPS // 2
    latitude = values.shape[1]
    mirrored = values[:, latitude - reach:, :][:, ::-1, ::-1]
    floor_rows = jnp.zeros((values.shape[0], reach, values.shape[2]), values.dtype)
    stacked = jnp.concatenate([floor_rows, values, mirrored], axis=1)
    return jnp.concatenate([stacked[:, :, -reach:], stacked, stacked[:, :, :reach]], axis=2)

def taps(padded, weights, height, width):
    source = padded.astype(jnp.float32)
    total = jnp.zeros((padded.shape[0], height, width), jnp.float32)
    for row_off in range(TAPS):
        for col_off in range(TAPS):
            piece = source[:, row_off:row_off + height, col_off:col_off + width]
            total = total + weights[:, row_off, col_off][:, None, None] * piece
    return total

def kernel_terms(padded, d_conv, height, width):
    source = padded.astype(jnp.float32)
    flat = d_conv.astype(jnp.float32)
    terms = []
    for row_off in range(TAPS):
        for col_off in range(TAPS):
            piece = source[:, row_off:row_off + height, col_off:col_off + width]
            terms.append(lax.optimization_barrier(jnp.sum(flat * piece, axis=(1, 2))))
    return jnp.stack(terms, axis=1).reshape(padded.shape[0], TAPS, TAPS)

def fold_term(fold_rows, weights, width):
    reach = TAPS // 2
    lines = []
    for depth in range(reach):
        total = jnp.zeros((fold_rows.shape[0], width), jnp.float32)
        for source in range(reach - depth):
            for col_off in range(TAPS):
                piece = fold_rows[:, source, col_off:col_off + width].astype(jnp.float32)
                total = total + weights[:, reach + 1 + depth + source, col_off][:, None] * piece
        lines.append(total)
    return jnp.stack(lines[::-1], axis=1)

def gelu_slope(hidden):
    return 0.5 * (1.0 + lax.erf(hidden * root_half)) + hidden * jnp.exp(-0.5 * hidden * hidden) * inv_root_tau

def cell_pass(convolved, residual, incoming, ocean, norm_gain, norm_shift, weight_in, weight_out):
    centre = lax.optimization_barrier(jnp.mean(convolved, axis=0, keepdims=True))
    centred = convolved - centre
    spread = lax.optimization_barrier(jnp.mean(centred * centred, axis=0, keepdims=True))
    rstd = lax.rsqrt(spread + epsilon)
    normed = centred * rstd
    lifted = (normed * norm_gain[:, None] + norm_shift[:, None]).astype(jnp.bfloat16)
    hidden = lax.dot_general(weight_in, lifted, (((0,), (0,)), ((), ())), preferred_element_type=jnp.float32)
    active = jax.nn.gelu(hidden, approximate=False).astype(jnp.bfloat16)
    projected = lax.dot_general(weight_out, active, (((0,), (0,)), ((), ())), preferred_element_type=jnp.float32)
    wet = ocean.astype(jnp.float32)[None, :]
    result = (wet * (residual.astype(jnp.float32) + projected)).astype(jnp.bfloat16)
    upstream = incoming.astype(jnp.float32) * wet
    d_active = jnp.dot(weight_out, upstream.astype(jnp.bfloat16), preferred_element_type=jnp.float32)
    d_hidden = (d_active * gelu_slope(hidden)).astype(jnp.bfloat16)
    d_lifted = jnp.dot(weight_in, d_hidden, preferred_element_type=jnp.float32)
    d_normed = d_lifted * norm_gain[:, None]
    first = lax.optimization_barrier(jnp.mean(d_normed, axis=0, keepdims=True))
    second = lax.optimization_barrier(jnp.mean(d_normed * normed, axis=0, keepdims=True))
    d_conv = (rstd * (d_normed - first - normed * second)).astype(jnp.bfloat16)
    return (result, upstream, d_conv)

def reference(snapshot, cotangent, ocean_mask, kernel, norm_gain, norm_shift, weight_in, weight_out):
    channels, latitude, longitude = snapshot.shape
    reach = TAPS // 2
    weights = kernel.astype(jnp.float32).reshape(channels, TAPS, TAPS)
    flipped = weights[:, ::-1, ::-1]
    padded = fold_pad(snapshot)
    count = LAT_DEV * longitude
    blocks = jnp.arange(latitude // LAT_DEV, dtype=jnp.int32)

    def forward_block(carry, block):
        start = (block * LAT_DEV).astype(jnp.int32)
        window = lax.dynamic_slice_in_dim(padded, start, LAT_DEV + 2 * reach, 1)
        convolved = taps(window, weights, LAT_DEV, longitude)
        residual = window[:, reach:reach + LAT_DEV, reach:reach + longitude]
        incoming = lax.dynamic_slice_in_dim(cotangent, start, LAT_DEV, 1)
        ocean = lax.dynamic_slice_in_dim(ocean_mask, start, LAT_DEV, 0)
        result, upstream, d_conv = cell_pass(convolved.reshape(channels, count), residual.reshape(channels, count), incoming.reshape(channels, count), ocean.reshape(count), norm_gain, norm_shift, weight_in, weight_out)
        d_conv = d_conv.reshape(channels, LAT_DEV, longitude)
        carry = carry + kernel_terms(window, d_conv, LAT_DEV, longitude)
        return (carry, (result.reshape(channels, LAT_DEV, longitude), upstream.reshape(channels, LAT_DEV, longitude), d_conv))
    kernel_grad, (results, upstreams, d_convs) = lax.scan(forward_block, jnp.zeros((channels, TAPS, TAPS), jnp.float32), blocks)

    def join(stack):
        return jnp.moveaxis(stack, 0, 1).reshape(channels, latitude, longitude)
    result = join(results)
    upstream = join(upstreams)
    d_conv = join(d_convs)
    d_padded = fold_pad(d_conv)
    fold_rows = d_padded[:, latitude + reach:, :]
    regular = jnp.concatenate([d_padded[:, :latitude + reach], jnp.zeros_like(fold_rows)], axis=1)

    def adjoint_block(block):
        start = (block * LAT_DEV).astype(jnp.int32)
        window = lax.dynamic_slice_in_dim(regular, start, LAT_DEV + 2 * reach, 1)
        return taps(window, flipped, LAT_DEV, longitude)
    adjoint = join(lax.map(adjoint_block, blocks))
    edge = fold_term(fold_rows, weights, longitude)
    adjoint = adjoint.at[:, latitude - reach:, :].add(edge)
    d_snapshot = (upstream + adjoint).astype(jnp.bfloat16)
    return (result, d_snapshot, kernel_grad.reshape(channels, TAPS * TAPS))
```

```python
import functools

import jax
import jax.numpy as jnp
from jax import lax
from jax.experimental import pallas as pl
from jax.experimental.pallas import tpu as pltpu
from jax.sharding import PartitionSpec as P

MESH = pl.DeviceIdType.MESH
F32 = jnp.float32
BF16 = jnp.bfloat16
TAPS = 7
REACH = 3
W = 128
SUB = 8

epsilon = 1e-06
root_half = 0.7071067811865476
inv_root_tau = 0.3989422804014327


class Dims:
    def __init__(self, levs, lons, channels, rows, hidden):
        self.levs, self.lons, self.channels, self.rows, self.hidden = levs, lons, channels, rows, hidden
        self.cl = channels // levs
        self.tile = rows // levs
        self.used = self.tile * self.cl
        self.block = -(-(self.used + 2 * self.tile) // 16) * 16
        self.groups = self.cl // SUB
        self.step = max(r for r in (8, 6, 4, 3) if rows % r == 0)
        self.packs = -(-rows // 32)
        self.core = 2
        self.zhi = 4 if lons == 32 else 2
        self.x = lons // (self.core * self.zhi)
        self.first = self.x * self.core


def lane_iota(shape=(SUB, W)):
    return lax.broadcasted_iota(jnp.int32, shape, 1)


def lev_peer(d, me, offset):
    return lax.rem(me + offset, d.levs)


def lon_targets(d):
    me = lax.axis_index("lon")
    n = d.lons
    mirror = n - 1 - me
    right, left = lax.rem(me + 1, n), lax.rem(me + n - 1, n)
    return me, (right, left), (mirror, lax.rem(mirror + 1, n), lax.rem(mirror + n - 1, n))


def signal(sem, where):
    pl.semaphore_signal(sem, inc=1, device_id=where, device_id_type=MESH)


def greet(d, sem):
    lev = lax.axis_index("lev")
    me, sides, mirrors = lon_targets(d)

    @pl.loop(1, d.levs)
    def _(s):
        signal(sem, {"lev": lev_peer(d, lev, s)})

    for side in sides:
        signal(sem, {"lon": side})
    for mirror in mirrors:

        @pl.when(mirror != me)
        def _(mirror=mirror):
            signal(sem, {"lon": mirror})


def met(d, sem, more=0):
    me, _, mirrors = lon_targets(d)
    own = sum(jnp.where(mirror == me, 1, 0) for mirror in mirrors)
    pl.semaphore_wait(sem, d.levs - 1 + 2 + len(mirrors) + more - own)


def edge_copies(d, hs, hr, fs, fr, sems):
    me, sides, mirrors = lon_targets(d)
    send, recv = sems
    for j, side in enumerate(sides):
        yield None, pltpu.make_async_remote_copy(
            src_ref=hs.at[j], dst_ref=hr.at[j], send_sem=send.at[j], recv_sem=recv.at[j],
            device_id={"lon": side}, device_id_type=MESH,
        ), None
    for j, mirror in enumerate(mirrors):
        yield mirror != me, pltpu.make_async_remote_copy(
            src_ref=fs, dst_ref=fr.at[j], send_sem=send.at[2 + j], recv_sem=recv.at[2 + j],
            device_id={"lon": mirror}, device_id_type=MESH,
        ), pltpu.make_async_copy(fs, fr.at[j], recv.at[2 + j])


def edge_start(d, *refs):
    for away, remote, own in edge_copies(d, *refs):
        if away is None:
            remote.start()
        else:
            pl.when(away)(remote.start)
            pl.when(jnp.logical_not(away))(own.start)


def edge_wait(d, *refs):
    for away, remote, own in edge_copies(d, *refs):
        if away is None:
            remote.wait()
        else:
            pl.when(away)(remote.wait)
            pl.when(jnp.logical_not(away))(own.wait)


def block_copy(d, me, offset, src, dst, send, recv, arriving=False):
    peer = lev_peer(d, me, offset)
    return pltpu.make_async_remote_copy(
        src_ref=src.at[peer],
        dst_ref=dst.at[peer if arriving else me],
        send_sem=send.at[peer],
        recv_sem=recv.at[peer if arriving else me],
        device_id={"lev": peer},
        device_id_type=MESH,
    )


def blocks_start(d, src, dst, send, recv):
    me = lax.axis_index("lev")

    @pl.loop(1, d.levs)
    def _(s):
        block_copy(d, me, s, src, dst, send, recv).start()

    dst[me] = src[me]


def blocks_arrive(d, src, dst, send, recv):
    me = lax.axis_index("lev")

    @pl.loop(1, d.levs)
    def _(s):
        block_copy(d, me, s, src, dst, send, recv, True).wait_recv()


def blocks_sent(d, src, dst, send, recv):
    me = lax.axis_index("lev")

    @pl.loop(1, d.levs)
    def _(s):
        block_copy(d, me, s, src, dst, send, recv).wait_send()


def pack_edges(d, rows, hs, fs, tail):
    slot = lane_iota() >> 2

    @pl.loop(0, d.groups)
    def _(g):
        for q in range(d.packs):
            last = jnp.zeros((SUB, W), F32)
            lead = jnp.zeros((SUB, W), F32)
            for r in range(32 * q, min(32 * q + 32, d.rows)):
                s = r - 32 * q
                v = rows[pl.ds(pl.multiple_of(r * d.cl + g * SUB, SUB), SUB), :]
                here = slot == s
                last = jnp.where(here, pltpu.roll(v, (4 * s - (W - REACH)) % W, 1), last)
                lead = jnp.where(here, pltpu.roll(v, 4 * s, 1) if s else v, lead)
            at = pl.ds(pl.multiple_of(q * d.cl + g * SUB, SUB), SUB)
            tail[0, at, :] = last
            tail[1, at, :] = lead

    hs[...] = tail[:, : hs.shape[1], :].astype(BF16)
    north = (d.rows - REACH) * d.cl
    fs[: REACH * d.cl, :] = rows[north : north + REACH * d.cl, :].astype(BF16)


def store_shifts(x, left, right, lane, put):
    put(REACH, x)
    for k in range(1, REACH + 1):
        put(REACH - k, pltpu.roll(jnp.where(lane >= W - k, left, x), k, 1))
        put(REACH + k, pltpu.roll(jnp.where(lane < k, right, x), W - k, 1))


def build_shifts(d, rows, hr, halo, out):
    halo[:, : hr.shape[1], :] = hr[...].astype(F32)
    lane = lane_iota()

    @pl.loop(0, d.groups)
    def _(g):
        for r in range(d.rows):
            q, s = divmod(r, 32)
            at = pl.ds(pl.multiple_of(q * d.cl + g * SUB, SUB), SUB)
            left = pltpu.roll(halo[0, at, :], (W - REACH - 4 * s) % W, 1)
            right = pltpu.roll(halo[1, at, :], (W - 4 * s) % W, 1) if s else halo[1, at, :]
            x = rows[pl.ds(pl.multiple_of(r * d.cl + g * SUB, SUB), SUB), :]
            to = pl.ds(pl.multiple_of((r + REACH) * d.cl + g * SUB, SUB), SUB)

            def put(b, value, to=to):
                out[b, to, :] = value

            store_shifts(x, left, right, lane, put)


def fold_shifts(d, fr, out, base):
    count = REACH * d.cl
    flip = lax.broadcasted_iota(jnp.int32, (W, W), 0) + lax.broadcasted_iota(jnp.int32, (W, W), 1) == W - 1
    flip = flip.astype(F32).astype(BF16)
    centre, left, right = (jnp.dot(fr[j], flip, preferred_element_type=F32) for j in range(3))
    lane = lane_iota()
    for m in range(REACH):
        for g in range(d.groups):
            src = (REACH - 1 - m) * d.cl + g * SUB
            to = base + m * d.cl + g * SUB

            def put(b, value, to=to):
                out[b, to : to + SUB, :] = value

            store_shifts(centre[src : src + SUB], left[src : src + SUB], right[src : src + SUB], lane, put)


def correlate(d, image, weights, out, flipped):
    blocks = d.rows // d.step

    @pl.loop(0, blocks * d.groups)
    def _(n):
        g = lax.rem(n, d.groups)
        top = n // d.groups * d.step
        acc = [jnp.zeros((SUB, W), F32) for _ in range(d.step)]
        for b in range(TAPS):
            near = TAPS - 1 - b if flipped else b
            lines = [
                image[near, pl.ds(pl.multiple_of((top + t) * d.cl + g * SUB, SUB), SUB), :]
                for t in range(d.step + TAPS - 1)
            ]
            for a in range(TAPS):
                w = weights[a * TAPS + b, pl.ds(pl.multiple_of(g * SUB, SUB), SUB), :]
                down = TAPS - 1 - a if flipped else a
                acc = [acc[i] + w * lines[i + down] for i in range(d.step)]
        for i in range(d.step):
            out[pl.ds(pl.multiple_of((top + i) * d.cl + g * SUB, SUB), SUB), :] = acc[i]


def tap_products(d, image, flat, grad):
    lane = lane_iota()
    grad[...] = jnp.zeros_like(grad)

    @pl.loop(0, TAPS * d.groups)
    def _(n):
        b = lax.rem(n, TAPS)
        g = n // TAPS
        acc = [jnp.zeros((SUB, W), F32) for _ in range(TAPS)]
        for block in range(d.rows // d.step):
            top = block * d.step
            lines = [
                image[b, pl.ds(pl.multiple_of((top + t) * d.cl + g * SUB, SUB), SUB), :]
                for t in range(d.step + TAPS - 1)
            ]
            for i in range(d.step):
                v = flat[pl.ds(pl.multiple_of((top + i) * d.cl + g * SUB, SUB), SUB), :]
                acc = [acc[a] + v * lines[i + a] for a in range(TAPS)]
        at = pl.ds(pl.multiple_of(g * SUB, SUB), SUB)
        total = grad[at, :]
        for a in range(TAPS):
            total = jnp.where(lane == a * TAPS + b, jnp.sum(acc[a], axis=1, keepdims=True), total)
        grad[at, :] = total


def forward_kernel(d, snap, kern, cbuf, rbuf, shifted, weights,
                   rows, conv, pad32, wide, tail, hs, hr, fs, fr, rs, cs,
                   edge_send, edge_recv, r_send, r_recv, c_send, c_recv):
    barrier = pltpu.get_barrier_semaphore()
    greet(d, barrier)
    lev = lax.axis_index("lev")
    for c in range(d.cl):
        rows[pl.ds(c, d.rows, stride=d.cl), :] = snap[c].astype(F32)
    fs[...] = jnp.zeros_like(fs)
    pack_edges(d, rows, hs, fs, tail)
    for k in range(d.levs):
        rs[k, : d.used, :] = rows[k * d.used : (k + 1) * d.used, :].astype(BF16)
        rs[k, d.used :, :] = jnp.zeros((d.block - d.used, W), BF16)
    met(d, barrier)
    edge = (hs, hr, fs, fr, (edge_send, edge_recv))
    edge_start(d, *edge)
    blocks_start(d, rs, rbuf, r_send, r_recv)

    wide[...] = kern[...].astype(F32)
    mine = wide[pl.ds(pl.multiple_of(lev * d.cl, SUB), d.cl), :]
    for t in range(TAPS * TAPS):
        weights[t] = jnp.broadcast_to(mine[:, t : t + 1], (d.cl, W))
    for b in range(TAPS):
        shifted[b, : REACH * d.cl, :] = jnp.zeros((REACH * d.cl, W), F32)

    edge_wait(d, *edge)
    build_shifts(d, rows, hr, tail, shifted)
    fold_shifts(d, fr, shifted, (REACH + d.rows) * d.cl)
    correlate(d, shifted, weights, conv, False)

    sub = lax.broadcasted_iota(jnp.int32, (d.block - d.used, W), 0)

    @pl.loop(0, d.levs)
    def _(k):
        offsets = jnp.zeros((d.block - d.used, W), F32)
        for r in range(d.tile):
            v = conv[pl.ds(pl.multiple_of(k * d.used + r * d.cl, SUB), d.cl), :]
            mean = jnp.sum(v, axis=0, keepdims=True) * (1.0 / d.cl)
            high = mean.astype(BF16).astype(F32)
            low = (mean - high).astype(BF16).astype(F32)
            pad32[r * d.cl : (r + 1) * d.cl, :] = v - (high + low)
            offsets = jnp.where(sub == 2 * r, high, jnp.where(sub == 2 * r + 1, low, offsets))
        pad32[d.used :, :] = offsets
        cs[k] = pad32[...].astype(BF16)

    blocks_start(d, cs, cbuf, c_send, c_recv)
    blocks_arrive(d, rs, rbuf, r_send, r_recv)
    blocks_arrive(d, cs, cbuf, c_send, c_recv)
    blocks_sent(d, rs, rbuf, r_send, r_recv)
    blocks_sent(d, cs, cbuf, c_send, c_recv)


def column_of(vector, out):
    for j in range(vector.shape[0]):
        n = vector.shape[1]
        line = jnp.broadcast_to(vector[j : j + 1, :], (W, n))
        out[j * n : (j + 1) * n, :] = jnp.transpose(line)


def cell_kernel(d, cbuf, rbuf, cot, mask, gain, shift, w_in, w_out, result, dsend, usend,
                gains, shifts, normed, rstds, lifted, upstream, projected, d_lifted, blocks):
    column_of(gain[...], gains)
    column_of(shift[...], shifts)
    for k in range(d.levs):
        v = cbuf[k].astype(F32)
        for r in range(d.tile):
            at = d.used + 2 * r
            normed[r, k * d.cl : (k + 1) * d.cl, :] = v[r * d.cl : (r + 1) * d.cl] + (v[at : at + 1] + v[at + 1 : at + 2])
    wet = mask[...].astype(F32)
    inv = 1.0 / d.channels
    for r in range(d.tile):
        v = normed[r]
        v = v - jnp.sum(v, axis=0, keepdims=True) * inv
        spread = jnp.sum(v * v, axis=0, keepdims=True) * inv
        rstd = lax.rsqrt(spread + epsilon)
        v = v * rstd
        normed[r] = v
        rstds[r : r + 1, :] = rstd
        cells = pl.ds(r * W, W)
        lifted[cells, :] = jnp.transpose(v * gains[...] + shifts[...]).astype(BF16)
        up = cot[r].astype(F32) * wet[r : r + 1, :]
        upstream[cells, :] = jnp.transpose(up).astype(BF16)
        for k in range(d.levs):
            blocks[k, r * d.cl : (r + 1) * d.cl, :] = up[k * d.cl : (k + 1) * d.cl]
    for k in range(d.levs):
        blocks[k, d.used :, :] = jnp.zeros((d.block - d.used, W), F32)
    usend[...] = blocks[...].astype(BF16)

    chunk = 256
    for n in range(d.hidden // chunk):
        f = slice(n * chunk, (n + 1) * chunk)
        hidden = jnp.dot(lifted[...], w_in[:, f], preferred_element_type=F32)
        d_active = lax.dot_general(upstream[...], w_out[f, :], (((1,), (1,)), ((), ())), preferred_element_type=F32)
        share = 0.5 * (1.0 + lax.erf(hidden * root_half))
        active = (hidden * share).astype(BF16)
        slope = share + hidden * jnp.exp(-0.5 * hidden * hidden) * inv_root_tau
        d_hidden = (d_active * slope).astype(BF16)
        p = jnp.dot(active, w_out[f, :], preferred_element_type=F32)
        q = lax.dot_general(w_in[:, f], d_hidden, (((1,), (1,)), ((), ())), preferred_element_type=F32)
        if n == 0:
            projected[...] = p
            d_lifted[...] = q
        else:
            projected[...] += p
            d_lifted[...] += q

    for k in range(d.levs):
        blocks[k] = rbuf[k].astype(F32)
    for r in range(d.tile):
        cells = slice(r * W, (r + 1) * W)
        out = jnp.transpose(projected[cells, :])
        for k in range(d.levs):
            part = slice(k * d.cl, (k + 1) * d.cl)
            d_lifted_part = blocks[k, r * d.cl : (r + 1) * d.cl, :] + out[part]
            shifts[part, :] = wet[r : r + 1, :] * d_lifted_part
        result[r] = shifts[...].astype(BF16)
        dn = d_lifted[:, cells] * gains[...]
        v = normed[r]
        mean = jnp.sum(dn, axis=0, keepdims=True) * inv
        along = jnp.sum(dn * v, axis=0, keepdims=True) * inv
        dc = rstds[r : r + 1, :] * (dn - mean - v * along)
        normed[r] = dc
    for r in range(d.tile):
        for k in range(d.levs):
            blocks[k, r * d.cl : (r + 1) * d.cl, :] = normed[r, k * d.cl : (k + 1) * d.cl, :]
    dsend[...] = blocks[...].astype(BF16)


def first_peer(d, lon, offset):
    z = lax.rem(lon // d.core, d.zhi)
    mine = lon // (d.core * d.zhi) * d.core + lax.rem(lon, d.core)
    theirs = lax.rem(mine + offset, d.first)
    peer = (theirs // d.core * d.zhi + z) * d.core + lax.rem(theirs, d.core)
    return mine, theirs, peer


def second_peer(d, lon, offset):
    mine = lax.rem(lon // d.core, d.zhi)
    theirs = lax.rem(mine + offset, d.zhi)
    return mine, theirs, lon + (theirs - mine) * d.core


def share_copy(d, peers, count, offset, src, dst, send, recv, arriving=False):
    mine, theirs, peer = peers(d, lax.axis_index("lon"), offset)
    return pltpu.make_async_remote_copy(
        src_ref=src, dst_ref=dst.at[theirs if arriving else mine], send_sem=send.at[theirs],
        recv_sem=recv.at[theirs if arriving else mine], device_id={"lon": peer}, device_id_type=MESH,
    )


def share_start(d, peers, count, src, dst, send, recv):
    mine, _, _ = peers(d, lax.axis_index("lon"), 1)
    for s in range(1, count):
        share_copy(d, peers, count, s, src, dst, send, recv).start()
    dst[mine] = src[...]


def share_wait(d, peers, count, src, dst, send, recv):
    for s in range(1, count):
        share_copy(d, peers, count, s, src, dst, send, recv, True).wait_recv()
    for s in range(1, count):
        share_copy(d, peers, count, s, src, dst, send, recv).wait_send()


def gather_copy(d, offset, src, dst, send, recv, arriving=False):
    me = lax.axis_index("lev")
    peer = lev_peer(d, me, offset)
    return pltpu.make_async_remote_copy(
        src_ref=src, dst_ref=dst.at[peer if arriving else me], send_sem=send.at[peer],
        recv_sem=recv.at[peer if arriving else me], device_id={"lev": peer}, device_id_type=MESH,
    )


def backward_kernel(d, dsend, usend, shifted, weights, out, grads,
                    rows, image, fold, tail, sums, hs, hr, fs, fr, dbuf, ubuf, grad, part1, total1, part2, total2,
                    edge_send, edge_recv, d_send, d_recv, u_send, u_recv, p1s, p1r, p2s, p2r, gs, gr):
    barrier = pltpu.get_barrier_semaphore()
    greet(d, barrier)
    lon = lax.axis_index("lon")
    lev = lax.axis_index("lev")
    for s in range(1, d.first):
        signal(barrier, {"lon": first_peer(d, lon, s)[2]})
    for s in range(1, d.zhi):
        signal(barrier, {"lon": second_peer(d, lon, s)[2]})
    fs[...] = jnp.zeros_like(fs)
    for b in range(TAPS):
        image[b, : REACH * d.cl, :] = jnp.zeros((REACH * d.cl, W), F32)
        image[b, (REACH + d.rows) * d.cl :, :] = jnp.zeros((REACH * d.cl, W), F32)
    met(d, barrier, d.first - 1 + d.zhi - 1)
    blocks_start(d, dsend, dbuf, d_send, d_recv)
    blocks_start(d, usend, ubuf, u_send, u_recv)

    blocks_arrive(d, dsend, dbuf, d_send, d_recv)
    for k in range(d.levs):
        rows[k * d.used : (k + 1) * d.used, :] = dbuf[k, : d.used, :].astype(F32)
    pack_edges(d, rows, hs, fs, tail)
    edge = (hs, hr, fs, fr, (edge_send, edge_recv))
    edge_start(d, *edge)
    tap_products(d, shifted, rows, grad)
    first = (d, first_peer, d.first, grad, part1, p1s, p1r)
    share_start(*first)

    edge_wait(d, *edge)
    build_shifts(d, rows, hr, tail, image)
    fold_shifts(d, fr, fold, 0)

    share_wait(*first)
    total1[...] = sum(part1[i] for i in range(d.first))
    second = (d, second_peer, d.zhi, total1, part2, p2s, p2r)
    share_start(*second)

    correlate(d, image, weights, sums, True)

    share_wait(*second)
    total2[...] = sum(part2[i] for i in range(d.zhi))
    for s in range(1, d.levs):
        gather_copy(d, s, total2, grads, gs, gr).start()
    grads[lev] = total2[...]

    for m in range(REACH):
        for g in range(d.groups):
            at = (d.rows - 1 - m) * d.cl + g * SUB
            acc = sums[at : at + SUB, :]
            for k in range(REACH - m):
                for b in range(TAPS):
                    w = weights[(REACH + 1 + m + k) * TAPS + b, g * SUB : (g + 1) * SUB, :]
                    acc = acc + w * fold[b, k * d.cl + g * SUB : k * d.cl + (g + 1) * SUB, :]
            sums[at : at + SUB, :] = acc
    blocks_arrive(d, usend, ubuf, u_send, u_recv)
    for k in range(d.levs):
        part = slice(k * d.used, (k + 1) * d.used)
        sums[part, :] = sums[part, :] + ubuf[k, : d.used, :].astype(F32)
    for c in range(d.cl):
        out[c] = sums[pl.ds(c, d.rows, stride=d.cl), :].astype(BF16)

    for s in range(1, d.levs):
        gather_copy(d, s, total2, grads, gs, gr, True).wait_recv()
    for s in range(1, d.levs):
        gather_copy(d, s, total2, grads, gs, gr).wait_send()
    blocks_sent(d, dsend, dbuf, d_send, d_recv)
    blocks_sent(d, usend, ubuf, u_send, u_recv)


VMEM = pl.BlockSpec(memory_space=pltpu.VMEM)
DMA = pltpu.SemaphoreType.DMA
LIMIT = 60 * 1024 * 1024


def params(number):
    return pltpu.CompilerParams(collective_id=number, has_side_effects=True, vmem_limit_bytes=LIMIT)


def shards(snapshot, cotangent, ocean_mask, kernel, norm_gain, norm_shift, weight_in, weight_out):
    levs, lons = lax.axis_size("lev"), lax.axis_size("lon")
    cl, rows, _ = snapshot.shape
    d = Dims(levs, lons, cl * levs, rows, weight_in.shape[1])
    sds = jax.ShapeDtypeStruct
    blocks = (d.levs, d.block, W)
    flat = (d.rows * d.cl, W)
    image = (TAPS, (d.rows + 2 * REACH) * d.cl, W)
    halo = (2, -(-d.packs * d.cl // 16) * 16, W)
    north = (-(-REACH * d.cl // 16) * 16, W)
    edge_scratch = [
        pltpu.VMEM(halo, BF16), pltpu.VMEM(halo, BF16), pltpu.VMEM(north, BF16), pltpu.VMEM((3, *north), BF16),
    ]
    cbuf, rbuf, shifted, weights = pl.pallas_call(
        functools.partial(forward_kernel, d),
        name="forward",
        out_shape=(sds(blocks, BF16), sds(blocks, BF16), sds(image, F32), sds((TAPS * TAPS, d.cl, W), F32)),
        in_specs=[VMEM] * 2,
        out_specs=(VMEM,) * 4,
        scratch_shapes=[
            pltpu.VMEM(flat, F32), pltpu.VMEM(flat, F32), pltpu.VMEM((d.block, W), F32),
            pltpu.VMEM((d.channels, TAPS * TAPS), F32), pltpu.VMEM(halo, F32), *edge_scratch,
            pltpu.VMEM(blocks, BF16), pltpu.VMEM(blocks, BF16),
            DMA((5,)), DMA((5,)), *[DMA((d.levs,))] * 4,
        ],
        compiler_params=params(0),
    )(snapshot, kernel)

    cells = d.tile * W
    result, dsend, usend = pl.pallas_call(
        functools.partial(cell_kernel, d),
        name="cells",
        out_shape=(sds((d.tile, d.channels, W), BF16), sds(blocks, BF16), sds(blocks, BF16)),
        in_specs=[VMEM] * 8,
        out_specs=(VMEM,) * 3,
        scratch_shapes=[
            pltpu.VMEM((d.channels, W), F32), pltpu.VMEM((d.channels, W), F32),
            pltpu.VMEM((d.tile, d.channels, W), F32), pltpu.VMEM((d.tile, W), F32),
            pltpu.VMEM((cells, d.channels), BF16), pltpu.VMEM((cells, d.channels), BF16),
            pltpu.VMEM((cells, d.channels), F32), pltpu.VMEM((d.channels, cells), F32),
            pltpu.VMEM(blocks, F32),
        ],
        compiler_params=pltpu.CompilerParams(vmem_limit_bytes=LIMIT),
    )(
        cbuf, rbuf, jnp.swapaxes(cotangent, 0, 1), ocean_mask,
        norm_gain.reshape(-1, min(W, d.channels)), norm_shift.reshape(-1, min(W, d.channels)), weight_in, weight_out,
    )

    share = (d.cl, W)
    d_snapshot, grads = pl.pallas_call(
        functools.partial(backward_kernel, d),
        name="backward",
        out_shape=(sds((d.cl, d.rows, W), BF16), sds((d.levs, *share), F32)),
        in_specs=[VMEM] * 4,
        out_specs=(VMEM,) * 2,
        scratch_shapes=[
            pltpu.VMEM(flat, F32), pltpu.VMEM(image, F32), pltpu.VMEM((TAPS, REACH * d.cl, W), F32),
            pltpu.VMEM(halo, F32), pltpu.VMEM(flat, F32), *edge_scratch,
            pltpu.VMEM(blocks, BF16), pltpu.VMEM(blocks, BF16),
            pltpu.VMEM(share, F32), pltpu.VMEM((d.first, *share), F32), pltpu.VMEM(share, F32),
            pltpu.VMEM((d.zhi, *share), F32), pltpu.VMEM(share, F32),
            DMA((5,)), DMA((5,)), *[DMA((d.levs,))] * 4,
            DMA((d.first,)), DMA((d.first,)), DMA((d.zhi,)), DMA((d.zhi,)), DMA((d.levs,)), DMA((d.levs,)),
        ],
        compiler_params=params(1),
    )(dsend, usend, shifted, weights)
    kernel_grad = grads.reshape(d.channels, W)[:, : TAPS * TAPS]
    return jnp.swapaxes(result, 0, 1), d_snapshot, kernel_grad


def solution(mesh):
    placed = (
        P("lev", None, "lon"),
        P(None, "lev", "lon"),
        P("lev", "lon"),
        P(),
        P(),
        P(),
        P(),
        P(),
    )
    return jax.shard_map(
        shards,
        mesh=mesh,
        in_specs=placed,
        out_specs=(P(None, "lev", "lon"), P("lev", None, "lon"), P()),
        check_vma=False,
    )
```

```python
import contextlib
import functools

import jax
import jax.numpy as jnp
from jax import lax
from jax.experimental import pallas as pl
from jax.experimental.pallas import tpu as pltpu
from jax.sharding import PartitionSpec as P

MESH = pl.DeviceIdType.MESH
F32 = jnp.float32
BF16 = jnp.bfloat16
TAPS = 7
REACH = 3
W = 128
SUB = 8

epsilon = 1e-06
root_half = 0.7071067811865476
inv_root_tau = 0.3989422804014327


TRACE = False


def phase(name):
    return jax.named_scope(name) if TRACE else contextlib.nullcontext()


class Dims:
    def __init__(self, levs, lons, channels, rows, hidden):
        self.levs, self.lons, self.channels, self.rows, self.hidden = levs, lons, channels, rows, hidden
        self.cl = channels // levs
        self.tile = rows // levs
        self.used = self.tile * self.cl
        self.block = -(-(self.used + 2 * self.tile) // 16) * 16
        self.groups = self.cl // SUB
        self.step = max(r for r in (8, 6, 4, 3) if rows % r == 0)
        self.packs = -(-rows // 32)
        self.core = 2
        self.zhi = 4 if lons == 32 else 2
        self.x = lons // (self.core * self.zhi)
        self.first = self.x * self.core


def lane_iota(shape=(SUB, W)):
    return lax.broadcasted_iota(jnp.int32, shape, 1)


def lev_peer(d, me, offset):
    return lax.rem(me + offset, d.levs)


def lon_targets(d):
    me = lax.axis_index("lon")
    n = d.lons
    mirror = n - 1 - me
    right, left = lax.rem(me + 1, n), lax.rem(me + n - 1, n)
    return me, (right, left), (mirror, lax.rem(mirror + 1, n), lax.rem(mirror + n - 1, n))


def signal(sem, where):
    pl.semaphore_signal(sem, inc=1, device_id=where, device_id_type=MESH)


def greet(d, sem):
    lev = lax.axis_index("lev")
    me, sides, mirrors = lon_targets(d)

    @pl.loop(1, d.levs)
    def _(s):
        signal(sem, {"lev": lev_peer(d, lev, s)})

    for side in sides:
        signal(sem, {"lon": side})
    for mirror in mirrors:

        @pl.when(mirror != me)
        def _(mirror=mirror):
            signal(sem, {"lon": mirror})


def met(d, sem, more=0):
    me, _, mirrors = lon_targets(d)
    own = sum(jnp.where(mirror == me, 1, 0) for mirror in mirrors)
    pl.semaphore_wait(sem, d.levs - 1 + 2 + len(mirrors) + more - own)


def edge_copies(d, hs, hr, fs, fr, sems):
    me, sides, mirrors = lon_targets(d)
    send, recv = sems
    for j, side in enumerate(sides):
        yield None, pltpu.make_async_remote_copy(
            src_ref=hs.at[j], dst_ref=hr.at[j], send_sem=send.at[j], recv_sem=recv.at[j],
            device_id={"lon": side}, device_id_type=MESH,
        ), None
    for j, mirror in enumerate(mirrors):
        yield mirror != me, pltpu.make_async_remote_copy(
            src_ref=fs, dst_ref=fr.at[j], send_sem=send.at[2 + j], recv_sem=recv.at[2 + j],
            device_id={"lon": mirror}, device_id_type=MESH,
        ), pltpu.make_async_copy(fs, fr.at[j], recv.at[2 + j])


def edge_start(d, *refs):
    for away, remote, own in edge_copies(d, *refs):
        if away is None:
            remote.start()
        else:
            pl.when(away)(remote.start)
            pl.when(jnp.logical_not(away))(own.start)


def edge_wait(d, *refs):
    for away, remote, own in edge_copies(d, *refs):
        if away is None:
            remote.wait()
        else:
            pl.when(away)(remote.wait)
            pl.when(jnp.logical_not(away))(own.wait)


def block_copy(d, me, offset, src, dst, send, recv, arriving=False):
    peer = lev_peer(d, me, offset)
    return pltpu.make_async_remote_copy(
        src_ref=src.at[peer],
        dst_ref=dst.at[peer if arriving else me],
        send_sem=send.at[peer],
        recv_sem=recv.at[peer if arriving else me],
        device_id={"lev": peer},
        device_id_type=MESH,
    )


def blocks_start(d, src, dst, send, recv):
    me = lax.axis_index("lev")

    @pl.loop(1, d.levs)
    def _(s):
        block_copy(d, me, s, src, dst, send, recv).start()

    dst[me] = src[me]


def blocks_arrive(d, src, dst, send, recv):
    me = lax.axis_index("lev")

    @pl.loop(1, d.levs)
    def _(s):
        block_copy(d, me, s, src, dst, send, recv, True).wait_recv()


def blocks_sent(d, src, dst, send, recv):
    me = lax.axis_index("lev")

    @pl.loop(1, d.levs)
    def _(s):
        block_copy(d, me, s, src, dst, send, recv).wait_send()


def pack_edges(d, rows, hs, fs, tail):
    slot = lane_iota() >> 2

    @pl.loop(0, d.groups)
    def _(g):
        for q in range(d.packs):
            last = jnp.zeros((SUB, W), F32)
            lead = jnp.zeros((SUB, W), F32)
            for r in range(32 * q, min(32 * q + 32, d.rows)):
                s = r - 32 * q
                v = rows[pl.ds(pl.multiple_of(r * d.cl + g * SUB, SUB), SUB), :]
                here = slot == s
                last = jnp.where(here, pltpu.roll(v, (4 * s - (W - REACH)) % W, 1), last)
                lead = jnp.where(here, pltpu.roll(v, 4 * s, 1) if s else v, lead)
            at = pl.ds(pl.multiple_of(q * d.cl + g * SUB, SUB), SUB)
            tail[0, at, :] = last
            tail[1, at, :] = lead

    hs[...] = tail[:, : hs.shape[1], :].astype(BF16)
    north = (d.rows - REACH) * d.cl
    fs[: REACH * d.cl, :] = rows[north : north + REACH * d.cl, :].astype(BF16)


def store_shifts(x, left, right, lane, put):
    put(REACH, x)
    for k in range(1, REACH + 1):
        put(REACH - k, pltpu.roll(jnp.where(lane >= W - k, left, x), k, 1))
        put(REACH + k, pltpu.roll(jnp.where(lane < k, right, x), W - k, 1))


def build_shifts(d, rows, hr, halo, out):
    halo[:, : hr.shape[1], :] = hr[...].astype(F32)
    lane = lane_iota()

    @pl.loop(0, d.groups)
    def _(g):
        for r in range(d.rows):
            q, s = divmod(r, 32)
            at = pl.ds(pl.multiple_of(q * d.cl + g * SUB, SUB), SUB)
            left = pltpu.roll(halo[0, at, :], (W - REACH - 4 * s) % W, 1)
            right = pltpu.roll(halo[1, at, :], (W - 4 * s) % W, 1) if s else halo[1, at, :]
            x = rows[pl.ds(pl.multiple_of(r * d.cl + g * SUB, SUB), SUB), :]
            to = pl.ds(pl.multiple_of((r + REACH) * d.cl + g * SUB, SUB), SUB)

            def put(b, value, to=to):
                out[b, to, :] = value

            store_shifts(x, left, right, lane, put)


def fold_shifts(d, fr, out, base):
    count = REACH * d.cl
    flip = lax.broadcasted_iota(jnp.int32, (W, W), 0) + lax.broadcasted_iota(jnp.int32, (W, W), 1) == W - 1
    flip = flip.astype(F32).astype(BF16)
    centre, left, right = (jnp.dot(fr[j], flip, preferred_element_type=F32) for j in range(3))
    lane = lane_iota()
    for m in range(REACH):
        for g in range(d.groups):
            src = (REACH - 1 - m) * d.cl + g * SUB
            to = base + m * d.cl + g * SUB

            def put(b, value, to=to):
                out[b, to : to + SUB, :] = value

            store_shifts(centre[src : src + SUB], left[src : src + SUB], right[src : src + SUB], lane, put)


def convolve_tile(d, image, weights, tile, pad32, sub):
    base = tile * d.used
    for g in range(d.groups):
        acc = [jnp.zeros((SUB, W), F32) for _ in range(d.tile)]
        for b in range(TAPS):
            lines = [
                image[b, pl.ds(pl.multiple_of(base + t * d.cl + g * SUB, SUB), SUB), :]
                for t in range(d.tile + TAPS - 1)
            ]
            for a in range(TAPS):
                w = weights[a * TAPS + b, g * SUB : (g + 1) * SUB, :]
                acc = [acc[i] + w * lines[i + a] for i in range(d.tile)]
        for i in range(d.tile):
            pad32[i * d.cl + g * SUB : i * d.cl + (g + 1) * SUB, :] = acc[i]
    offsets = jnp.zeros((d.block - d.used, W), F32)
    for r in range(d.tile):
        here = slice(r * d.cl, (r + 1) * d.cl)
        v = pad32[here, :]
        mean = jnp.sum(v, axis=0, keepdims=True) * (1.0 / d.cl)
        high = mean.astype(BF16).astype(F32)
        low = (mean - high).astype(BF16).astype(F32)
        pad32[here, :] = v - (high + low)
        offsets = jnp.where(sub == 2 * r, high, jnp.where(sub == 2 * r + 1, low, offsets))
    pad32[d.used :, :] = offsets


def correlate(d, image, weights, out, flipped):
    blocks = d.rows // d.step

    @pl.loop(0, blocks * d.groups)
    def _(n):
        g = lax.rem(n, d.groups)
        top = n // d.groups * d.step
        acc = [jnp.zeros((SUB, W), F32) for _ in range(d.step)]
        for b in range(TAPS):
            near = TAPS - 1 - b if flipped else b
            lines = [
                image[near, pl.ds(pl.multiple_of((top + t) * d.cl + g * SUB, SUB), SUB), :]
                for t in range(d.step + TAPS - 1)
            ]
            for a in range(TAPS):
                w = weights[a * TAPS + b, pl.ds(pl.multiple_of(g * SUB, SUB), SUB), :]
                down = TAPS - 1 - a if flipped else a
                acc = [acc[i] + w * lines[i + down] for i in range(d.step)]
        for i in range(d.step):
            out[pl.ds(pl.multiple_of((top + i) * d.cl + g * SUB, SUB), SUB), :] = acc[i]


def tap_products(d, image, flat, grad):
    lane = lane_iota()
    grad[...] = jnp.zeros_like(grad)

    @pl.loop(0, TAPS * d.groups)
    def _(n):
        b = lax.rem(n, TAPS)
        g = n // TAPS
        acc = [jnp.zeros((SUB, W), F32) for _ in range(TAPS)]
        for block in range(d.rows // d.step):
            top = block * d.step
            lines = [
                image[b, pl.ds(pl.multiple_of((top + t) * d.cl + g * SUB, SUB), SUB), :]
                for t in range(d.step + TAPS - 1)
            ]
            for i in range(d.step):
                v = flat[pl.ds(pl.multiple_of((top + i) * d.cl + g * SUB, SUB), SUB), :]
                acc = [acc[a] + v * lines[i + a] for a in range(TAPS)]
        at = pl.ds(pl.multiple_of(g * SUB, SUB), SUB)
        total = grad[at, :]
        for a in range(TAPS):
            total = jnp.where(lane == a * TAPS + b, jnp.sum(acc[a], axis=1, keepdims=True), total)
        grad[at, :] = total


def column_of(vector, out):
    for j in range(vector.shape[0]):
        n = vector.shape[1]
        line = jnp.broadcast_to(vector[j : j + 1, :], (W, n))
        out[j * n : (j + 1) * n, :] = jnp.transpose(line)


def first_peer(d, lon, offset):
    z = lax.rem(lon // d.core, d.zhi)
    mine = lon // (d.core * d.zhi) * d.core + lax.rem(lon, d.core)
    theirs = lax.rem(mine + offset, d.first)
    peer = (theirs // d.core * d.zhi + z) * d.core + lax.rem(theirs, d.core)
    return mine, theirs, peer


def second_peer(d, lon, offset):
    mine = lax.rem(lon // d.core, d.zhi)
    theirs = lax.rem(mine + offset, d.zhi)
    return mine, theirs, lon + (theirs - mine) * d.core


def share_copy(d, peers, count, offset, src, dst, send, recv, arriving=False):
    mine, theirs, peer = peers(d, lax.axis_index("lon"), offset)
    return pltpu.make_async_remote_copy(
        src_ref=src, dst_ref=dst.at[theirs if arriving else mine], send_sem=send.at[theirs],
        recv_sem=recv.at[theirs if arriving else mine], device_id={"lon": peer}, device_id_type=MESH,
    )


def share_start(d, peers, count, src, dst, send, recv):
    mine, _, _ = peers(d, lax.axis_index("lon"), 1)
    for s in range(1, count):
        share_copy(d, peers, count, s, src, dst, send, recv).start()
    dst[mine] = src[...]


def share_wait(d, peers, count, src, dst, send, recv):
    for s in range(1, count):
        share_copy(d, peers, count, s, src, dst, send, recv, True).wait_recv()
    for s in range(1, count):
        share_copy(d, peers, count, s, src, dst, send, recv).wait_send()


def gather_copy(d, offset, src, dst, send, recv, arriving=False):
    me = lax.axis_index("lev")
    peer = lev_peer(d, me, offset)
    return pltpu.make_async_remote_copy(
        src_ref=src, dst_ref=dst.at[peer if arriving else me], send_sem=send.at[peer],
        recv_sem=recv.at[peer if arriving else me], device_id={"lev": peer}, device_id_type=MESH,
    )


def block_kernel(d, snap, kern, cot, mask, gain, shift, w_in_hbm, w_out_hbm, result, out, grads,
                 rows, pad32, wide, tail, shifted, weights, image, fold, sums,
                 gains, shifts, normed, rstds, lifted, upstream, projected, d_lifted, blocks, w_in, w_out,
                 grad, part1, total1, part2, total2, gathered, gflat,
                 hs, hr, fs, fr, hs2, hr2, fs2, fr2, rs, rbuf, cs, cbuf, us, ubuf, ds, dbuf,
                 w_sem, e_send, e_recv, e2_send, e2_recv, r_send, r_recv, c_send, c_recv, u_send, u_recv, d_send, d_recv,
                 p1s, p1r, p2s, p2r, gs, gr):
    lev, lon = lax.axis_index("lev"), lax.axis_index("lon")
    barrier = pltpu.get_barrier_semaphore()
    greet(d, barrier)
    for s in range(1, d.first):
        signal(barrier, {"lon": first_peer(d, lon, s)[2]})
    for s in range(1, d.zhi):
        signal(barrier, {"lon": second_peer(d, lon, s)[2]})
    w_copies = [pltpu.make_async_copy(w_in_hbm, w_in, w_sem.at[0]), pltpu.make_async_copy(w_out_hbm, w_out, w_sem.at[1])]
    for copy in w_copies:
        copy.start()
    edge = (hs, hr, fs, fr, (e_send, e_recv))
    edge2 = (hs2, hr2, fs2, fr2, (e2_send, e2_recv))
    residual = (d, rs, rbuf, r_send, r_recv)
    forward = (d, cs, cbuf, c_send, c_recv)
    upward = (d, us, ubuf, u_send, u_recv)
    backward = (d, ds, dbuf, d_send, d_recv)

    with phase("prep"):
        for c in range(d.cl):
            rows[pl.ds(c, d.rows, stride=d.cl), :] = snap[c].astype(F32)
        fs[...] = jnp.zeros_like(fs)
        fs2[...] = jnp.zeros_like(fs2)
        pack_edges(d, rows, hs, fs, tail)
        for k in range(d.levs):
            rs[k] = rows[k * d.used : (k + 1) * d.used, :].astype(BF16)
    with phase("meet"):
        met(d, barrier, d.first - 1 + d.zhi - 1)
    edge_start(d, *edge)
    blocks_start(*residual)

    with phase("weights"):
        wide[...] = jnp.zeros_like(wide)
        wide[: TAPS * TAPS, :] = kern[...].astype(F32)
        for j in range(0, d.channels, W):
            n = min(W, d.channels - j)
            gflat[j : j + n, :] = jnp.transpose(wide[:, j : j + n])
        mine = gflat[pl.ds(pl.multiple_of(lev * d.cl, SUB), d.cl), :]
        for t in range(TAPS * TAPS):
            weights[t] = jnp.broadcast_to(mine[:, t : t + 1], (d.cl, W))
        for b in range(TAPS):
            shifted[b, : REACH * d.cl, :] = jnp.zeros((REACH * d.cl, W), F32)
            image[b, : REACH * d.cl, :] = jnp.zeros((REACH * d.cl, W), F32)
            image[b, (REACH + d.rows) * d.cl :, :] = jnp.zeros((REACH * d.cl, W), F32)
        column_of(gain[...], gains)
        column_of(shift[...], shifts)
        wet = mask[...].astype(F32)
        for r in range(d.tile):
            up = cot[r].astype(F32) * wet[r : r + 1, :]
            upstream[r * W : (r + 1) * W, :] = jnp.transpose(up).astype(BF16)
            for k in range(d.levs):
                blocks[k, r * d.cl : (r + 1) * d.cl, :] = up[k * d.cl : (k + 1) * d.cl]
        for k in range(d.levs):
            us[k] = blocks[k, : d.used, :].astype(BF16)

    with phase("edge_wait"):
        edge_wait(d, *edge)
    with phase("shifts"):
        build_shifts(d, rows, hr, tail, shifted)
        fold_shifts(d, fr, shifted, (REACH + d.rows) * d.cl)

    with phase("conv"):
        sub = lax.broadcasted_iota(jnp.int32, (d.block - d.used, W), 0)

        @pl.loop(1, d.levs + 1)
        def _(s):
            peer = lev_peer(d, lev, s)
            convolve_tile(d, shifted, weights, peer, pad32, sub)
            cs[peer] = pad32[...].astype(BF16)

            @pl.when(s < d.levs)
            def _():
                block_copy(d, lev, s, cs, cbuf, c_send, c_recv).start()

        cbuf[lev] = cs[lev]

    for copy in w_copies:
        copy.wait()
    with phase("conv_wait"):
        blocks_arrive(*forward)
    blocks_start(*upward)

    with phase("norm"):
        for k in range(d.levs):
            v = cbuf[k].astype(F32)
            for r in range(d.tile):
                at = d.used + 2 * r
                normed[r, k * d.cl : (k + 1) * d.cl, :] = v[r * d.cl : (r + 1) * d.cl] + (v[at : at + 1] + v[at + 1 : at + 2])
        inv = 1.0 / d.channels
        for r in range(d.tile):
            v = normed[r]
            v = v - jnp.sum(v, axis=0, keepdims=True) * inv
            spread = jnp.sum(v * v, axis=0, keepdims=True) * inv
            rstd = lax.rsqrt(spread + epsilon)
            v = v * rstd
            normed[r] = v
            rstds[r : r + 1, :] = rstd
            lifted[r * W : (r + 1) * W, :] = jnp.transpose(v * gains[...] + shifts[...]).astype(BF16)

    with phase("mlp"):
        chunk = 256
        for n in range(d.hidden // chunk):
            f = slice(n * chunk, (n + 1) * chunk)
            hidden = jnp.dot(lifted[...], w_in[:, f], preferred_element_type=F32)
            d_active = lax.dot_general(upstream[...], w_out[f, :], (((1,), (1,)), ((), ())), preferred_element_type=F32)
            share = 0.5 * (1.0 + lax.erf(hidden * root_half))
            active = (hidden * share).astype(BF16)
            slope = share + hidden * jnp.exp(-0.5 * hidden * hidden) * inv_root_tau
            d_hidden = (d_active * slope).astype(BF16)
            p = jnp.dot(active, w_out[f, :], preferred_element_type=F32)
            q = lax.dot_general(w_in[:, f], d_hidden, (((1,), (1,)), ((), ())), preferred_element_type=F32)
            if n == 0:
                projected[...] = p
                d_lifted[...] = q
            else:
                projected[...] += p
                d_lifted[...] += q

    with phase("dconv"):
        for r in range(d.tile):
            dn = d_lifted[:, r * W : (r + 1) * W] * gains[...]
            v = normed[r]
            mean = jnp.sum(dn, axis=0, keepdims=True) * inv
            along = jnp.sum(dn * v, axis=0, keepdims=True) * inv
            normed[r] = rstds[r : r + 1, :] * (dn - mean - v * along)
            for k in range(d.levs):
                blocks[k, r * d.cl : (r + 1) * d.cl, :] = normed[r, k * d.cl : (k + 1) * d.cl, :]
        for k in range(d.levs):
            ds[k] = blocks[k, : d.used, :].astype(BF16)
    blocks_start(*backward)

    with phase("result"):
        blocks_arrive(*residual)
        for k in range(d.levs):
            blocks[k, : d.used, :] = rbuf[k].astype(F32)
        for r in range(d.tile):
            moved = jnp.transpose(projected[r * W : (r + 1) * W, :])
            for k in range(d.levs):
                part = slice(k * d.cl, (k + 1) * d.cl)
                shifts[part, :] = wet[r : r + 1, :] * (blocks[k, r * d.cl : (r + 1) * d.cl, :] + moved[part])
            result[r] = shifts[...].astype(BF16)

    with phase("d_wait"):
        blocks_arrive(*backward)
    with phase("pack2"):
        for k in range(d.levs):
            rows[k * d.used : (k + 1) * d.used, :] = dbuf[k].astype(F32)
        pack_edges(d, rows, hs2, fs2, tail)
    edge_start(d, *edge2)
    with phase("grad"):
        tap_products(d, shifted, rows, grad)
    first = (d, first_peer, d.first, grad, part1, p1s, p1r)
    share_start(*first)

    with phase("edge2_wait"):
        edge_wait(d, *edge2)
    with phase("shifts2"):
        build_shifts(d, rows, hr2, tail, image)
        fold_shifts(d, fr2, fold, 0)

    with phase("share1_wait"):
        share_wait(*first)
    total1[...] = sum(part1[i] for i in range(d.first))
    second = (d, second_peer, d.zhi, total1, part2, p2s, p2r)
    share_start(*second)

    with phase("adjoint"):
        correlate(d, image, weights, sums, True)

    with phase("share2_wait"):
        share_wait(*second)
    total2[...] = sum(part2[i] for i in range(d.zhi))
    for s in range(1, d.levs):
        gather_copy(d, s, total2, gathered, gs, gr).start()
    gathered[lev] = total2[...]

    with phase("edge_term"):
        for m in range(REACH):
            for g in range(d.groups):
                at = (d.rows - 1 - m) * d.cl + g * SUB
                acc = sums[at : at + SUB, :]
                for k in range(REACH - m):
                    for b in range(TAPS):
                        w = weights[(REACH + 1 + m + k) * TAPS + b, g * SUB : (g + 1) * SUB, :]
                        acc = acc + w * fold[b, k * d.cl + g * SUB : k * d.cl + (g + 1) * SUB, :]
                sums[at : at + SUB, :] = acc
    with phase("u_wait"):
        blocks_arrive(*upward)
    with phase("finish"):
        for k in range(d.levs):
            part = slice(k * d.used, (k + 1) * d.used)
            sums[part, :] = sums[part, :] + ubuf[k].astype(F32)
        for c in range(d.cl):
            out[c] = sums[pl.ds(c, d.rows, stride=d.cl), :].astype(BF16)

    with phase("gather_wait"):
        for s in range(1, d.levs):
            gather_copy(d, s, total2, gathered, gs, gr, True).wait_recv()
    for k in range(d.levs):
        gflat[k * d.cl : (k + 1) * d.cl, :] = gathered[k]
    for j in range(0, d.channels, W):
        n = min(W, d.channels - j)
        grads[:, j : j + n] = jnp.transpose(gflat[j : j + n, :])[: TAPS * TAPS]
    for s in range(1, d.levs):
        gather_copy(d, s, total2, gathered, gs, gr).wait_send()
    blocks_sent(*residual)
    blocks_sent(*forward)
    blocks_sent(*upward)
    blocks_sent(*backward)


VMEM = pl.BlockSpec(memory_space=pltpu.VMEM)
ANY = pl.BlockSpec(memory_space=pl.ANY)
DMA = pltpu.SemaphoreType.DMA
LIMIT = 60 * 1024 * 1024


def shards(snapshot, cotangent, ocean_mask, kernel, norm_gain, norm_shift, weight_in, weight_out):
    levs, lons = lax.axis_size("lev"), lax.axis_size("lon")
    cl, rows, _ = snapshot.shape
    d = Dims(levs, lons, cl * levs, rows, weight_in.shape[1])
    sds = jax.ShapeDtypeStruct
    f32 = lambda *shape: pltpu.VMEM(shape, F32)
    b16 = lambda *shape: pltpu.VMEM(shape, BF16)
    flat = (d.rows * d.cl, W)
    image = (TAPS, (d.rows + 2 * REACH) * d.cl, W)
    halo = (2, -(-d.packs * d.cl // 16) * 16, W)
    north = (-(-REACH * d.cl // 16) * 16, W)
    cells = d.tile * W
    share = (d.cl, W)
    result, d_snapshot, grads = pl.pallas_call(
        functools.partial(block_kernel, d),
        name="block",
        out_shape=(
            sds((d.tile, d.channels, W), BF16), sds((d.cl, d.rows, W), BF16), sds((TAPS * TAPS, d.channels), F32),
        ),
        in_specs=[VMEM] * 6 + [ANY] * 2,
        out_specs=(VMEM,) * 3,
        scratch_shapes=[
            f32(*flat), f32(d.block, W), f32(W, d.channels), f32(*halo), f32(*image), f32(TAPS * TAPS, d.cl, W),
            f32(*image), f32(TAPS, REACH * d.cl, W), f32(*flat),
            f32(d.channels, W), f32(d.channels, W), f32(d.tile, d.channels, W), f32(d.tile, W),
            b16(cells, d.channels), b16(cells, d.channels), f32(cells, d.channels), f32(d.channels, cells),
            f32(d.levs, d.block, W), b16(*weight_in.shape), b16(*weight_out.shape),
            f32(*share), f32(d.first, *share), f32(*share), f32(d.zhi, *share), f32(*share),
            f32(d.levs, *share), f32(d.channels, W),
            *[b16(*halo), b16(*halo), b16(*north), b16(3, *north)] * 2,
            b16(d.levs, d.used, W), b16(d.levs, d.used, W), b16(d.levs, d.block, W), b16(d.levs, d.block, W),
            *[b16(d.levs, d.used, W)] * 4,
            DMA((2,)), *[DMA((5,))] * 4, *[DMA((d.levs,))] * 8,
            DMA((d.first,)), DMA((d.first,)), DMA((d.zhi,)), DMA((d.zhi,)), DMA((d.levs,)), DMA((d.levs,)),
        ],
        compiler_params=pltpu.CompilerParams(collective_id=0, has_side_effects=True, vmem_limit_bytes=LIMIT),
    )(
        snapshot, kernel.T, jnp.swapaxes(cotangent, 0, 1), ocean_mask,
        norm_gain.reshape(-1, min(W, d.channels)), norm_shift.reshape(-1, min(W, d.channels)), weight_in, weight_out,
    )
    return jnp.swapaxes(result, 0, 1), d_snapshot, grads.T


def solution(mesh):
    placed = (
        P("lev", None, "lon"),
        P(None, "lev", "lon"),
        P("lev", "lon"),
        P(),
        P(),
        P(),
        P(),
        P(),
    )
    return jax.shard_map(
        shards,
        mesh=mesh,
        in_specs=placed,
        out_specs=(P(None, "lev", "lon"), P("lev", None, "lon"), P()),
        check_vma=False,
    )
```

```python
import contextlib
import functools

import jax
import jax.numpy as jnp
from jax import lax
from jax.experimental import pallas as pl
from jax.experimental.pallas import tpu as pltpu
from jax.sharding import PartitionSpec as P

MESH = pl.DeviceIdType.MESH
F32 = jnp.float32
BF16 = jnp.bfloat16
TAPS = 7
REACH = 3
W = 128
SUB = 8

epsilon = 1e-06
root_half = 0.7071067811865476
inv_root_tau = 0.3989422804014327


TRACE = False


def phase(name):
    return jax.named_scope(name) if TRACE else contextlib.nullcontext()


class Dims:
    def __init__(self, levs, lons, channels, rows, hidden):
        self.levs, self.lons, self.channels, self.rows, self.hidden = levs, lons, channels, rows, hidden
        self.cl = channels // levs
        self.tile = rows // levs
        self.used = self.tile * self.cl
        self.block = -(-(self.used + 2 * self.tile) // 16) * 16
        self.groups = self.cl // SUB
        self.step = max(r for r in (8, 6, 4, 3) if rows % r == 0)
        self.packs = -(-rows // 16)
        self.core = 2
        self.zhi = 4 if lons == 32 else 2
        self.x = lons // (self.core * self.zhi)
        self.first = self.x * self.core


def lane_iota(shape=(SUB, W)):
    return lax.broadcasted_iota(jnp.int32, shape, 1)


def lev_peer(d, me, offset):
    return lax.rem(me + offset, d.levs)


def lon_targets(d):
    me = lax.axis_index("lon")
    n = d.lons
    mirror = n - 1 - me
    right, left = lax.rem(me + 1, n), lax.rem(me + n - 1, n)
    return me, (right, left), (mirror, lax.rem(mirror + 1, n), lax.rem(mirror + n - 1, n))


def signal(sem, where):
    pl.semaphore_signal(sem, inc=1, device_id=where, device_id_type=MESH)


def greet(d, sem):
    lev = lax.axis_index("lev")
    me, sides, mirrors = lon_targets(d)

    @pl.loop(1, d.levs)
    def _(s):
        signal(sem, {"lev": lev_peer(d, lev, s)})

    for side in sides:
        signal(sem, {"lon": side})
    for mirror in mirrors:

        @pl.when(mirror != me)
        def _(mirror=mirror):
            signal(sem, {"lon": mirror})


def met(d, sem, more=0):
    me, _, mirrors = lon_targets(d)
    own = sum(jnp.where(mirror == me, 1, 0) for mirror in mirrors)
    pl.semaphore_wait(sem, d.levs - 1 + 2 + len(mirrors) + more - own)


def edge_copies(d, hs, hr, fs, fr, sems):
    me, sides, mirrors = lon_targets(d)
    send, recv = sems
    for j, side in enumerate(sides):
        yield None, pltpu.make_async_remote_copy(
            src_ref=hs, dst_ref=hr.at[j], send_sem=send.at[j], recv_sem=recv.at[j],
            device_id={"lon": side}, device_id_type=MESH,
        ), None
    for j, mirror in enumerate(mirrors):
        yield mirror != me, pltpu.make_async_remote_copy(
            src_ref=fs, dst_ref=fr.at[j], send_sem=send.at[2 + j], recv_sem=recv.at[2 + j],
            device_id={"lon": mirror}, device_id_type=MESH,
        ), pltpu.make_async_copy(fs, fr.at[j], recv.at[2 + j])


def edge_start(d, *refs):
    for away, remote, own in edge_copies(d, *refs):
        if away is None:
            remote.start()
        else:
            pl.when(away)(remote.start)
            pl.when(jnp.logical_not(away))(own.start)


def edge_wait(d, *refs):
    for away, remote, own in edge_copies(d, *refs):
        if away is None:
            remote.wait()
        else:
            pl.when(away)(remote.wait)
            pl.when(jnp.logical_not(away))(own.wait)


def block_copy(d, me, offset, src, dst, send, recv, arriving=False):
    peer = lev_peer(d, me, offset)
    return pltpu.make_async_remote_copy(
        src_ref=src.at[peer],
        dst_ref=dst.at[peer if arriving else me],
        send_sem=send.at[peer],
        recv_sem=recv.at[peer if arriving else me],
        device_id={"lev": peer},
        device_id_type=MESH,
    )


def blocks_start(d, src, dst, send, recv, low=1, high=None):
    me = lax.axis_index("lev")

    @pl.loop(low, high or d.levs)
    def _(s):
        block_copy(d, me, s, src, dst, send, recv).start()

    if low == 1:
        dst[me] = src[me]


def blocks_arrive(d, src, dst, send, recv):
    me = lax.axis_index("lev")

    @pl.loop(1, d.levs)
    def _(s):
        block_copy(d, me, s, src, dst, send, recv, True).wait_recv()


def blocks_sent(d, src, dst, send, recv):
    me = lax.axis_index("lev")

    @pl.loop(1, d.levs)
    def _(s):
        block_copy(d, me, s, src, dst, send, recv).wait_send()


def pack_edges(d, rows, hs, fs, tail):
    slot = lane_iota() >> 3

    @pl.loop(0, d.groups)
    def _(g):
        for q in range(d.packs):
            both = jnp.zeros((SUB, W), F32)
            for r in range(16 * q, min(16 * q + 16, d.rows)):
                s = r - 16 * q
                v = rows[pl.ds(pl.multiple_of(r * d.cl + g * SUB, SUB), SUB), :]
                both = jnp.where(slot == s, pltpu.roll(v, (8 * s - (W - REACH)) % W, 1), both)
            tail[pl.ds(pl.multiple_of(q * d.cl + g * SUB, SUB), SUB), :] = both

    hs[...] = tail[...].astype(BF16)
    north = (d.rows - REACH) * d.cl
    fs[: REACH * d.cl, :] = rows[north : north + REACH * d.cl, :].astype(BF16)


def moves():
    row = lax.broadcasted_iota(jnp.int32, (2 * W, W), 0)
    column = lax.broadcasted_iota(jnp.int32, (2 * W, W), 1)
    for b in (0, 1, 2, 4, 5, 6):
        source = column + (b - REACH)
        yield jnp.where(row == jnp.where(source < 0, source + 2 * W, source), 1.0, 0.0).astype(BF16)


def build_shifts(d, rows, hr, halo, padded, both, move, out):
    west = (lax.broadcasted_iota(jnp.int32, both.shape, 1) & 7) < REACH
    both[...] = jnp.where(west, hr[0].astype(F32), hr[1].astype(F32))

    @pl.loop(0, d.groups)
    def _(g):
        for r in range(d.rows):
            q, s = divmod(r, 16)
            v = both[pl.ds(pl.multiple_of(q * d.cl + g * SUB, SUB), SUB), :]
            to = pl.ds(pl.multiple_of(r * d.cl + g * SUB, SUB), SUB)
            halo[to, :] = pltpu.roll(v, (W - REACH - 8 * s) % W, 1)

    count = d.rows * d.cl
    step = count // 3

    @pl.loop(0, 3)
    def _(n):
        here = pl.ds(pl.multiple_of(n * step, SUB), step)
        to = pl.ds(pl.multiple_of(REACH * d.cl + n * step, SUB), step)
        x = rows[here, :]
        out[REACH, to, :] = x
        padded[:step, :W] = x.astype(BF16)
        padded[:step, W:] = halo[here, :].astype(BF16)
        for j in range(3):
            moved = jnp.dot(padded[:step, :], move[:, 2 * j * W : 2 * (j + 1) * W], preferred_element_type=F32)
            for i in range(2):
                b = (0, 1, 2, 4, 5, 6)[2 * j + i]
                out[b, to, :] = moved[:, i * W : (i + 1) * W]


def fold_shifts(d, fr, padded, both, move, out, base):
    count = REACH * d.cl
    flip = lax.broadcasted_iota(jnp.int32, (W, W), 0) + lax.broadcasted_iota(jnp.int32, (W, W), 1) == W - 1
    flip = flip.astype(F32).astype(BF16)
    centre, left, right = (jnp.dot(fr[j], flip, preferred_element_type=F32) for j in range(3))
    low = lax.broadcasted_iota(jnp.int32, (d.cl, W), 1) < W // 2
    for m in range(REACH):
        src = slice((REACH - 1 - m) * d.cl, (REACH - m) * d.cl)
        out[REACH, base + m * d.cl : base + (m + 1) * d.cl, :] = centre[src]
        both[m * d.cl : (m + 1) * d.cl, :] = jnp.where(low, right[src], left[src])
    padded[:count, :W] = out[REACH, base : base + count, :].astype(BF16)
    padded[:count, W:] = both[:count, :].astype(BF16)
    for j in range(3):
        moved = jnp.dot(padded[:count, :], move[:, 2 * j * W : 2 * (j + 1) * W], preferred_element_type=F32)
        for i in range(2):
            b = (0, 1, 2, 4, 5, 6)[2 * j + i]
            out[b, base : base + count, :] = moved[:, i * W : (i + 1) * W]


def convolve_tile(d, image, weights, tile, pad32, sub):
    base = tile * d.used
    for g in range(d.groups):
        acc = [jnp.zeros((SUB, W), F32) for _ in range(d.tile)]
        for b in range(TAPS):
            lines = [
                image[b, pl.ds(pl.multiple_of(base + t * d.cl + g * SUB, SUB), SUB), :]
                for t in range(d.tile + TAPS - 1)
            ]
            for a in range(TAPS):
                w = weights[a * TAPS + b, g * SUB : (g + 1) * SUB, :]
                acc = [acc[i] + w * lines[i + a] for i in range(d.tile)]
        for i in range(d.tile):
            pad32[i * d.cl + g * SUB : i * d.cl + (g + 1) * SUB, :] = acc[i]
    offsets = jnp.zeros((d.block - d.used, W), F32)
    for r in range(d.tile):
        here = slice(r * d.cl, (r + 1) * d.cl)
        v = pad32[here, :]
        mean = jnp.sum(v, axis=0, keepdims=True) * (1.0 / d.cl)
        high = mean.astype(BF16).astype(F32)
        low = (mean - high).astype(BF16).astype(F32)
        pad32[here, :] = v - (high + low)
        offsets = jnp.where(sub == 2 * r, high, jnp.where(sub == 2 * r + 1, low, offsets))
    pad32[d.used :, :] = offsets


def correlate(d, image, weights, out, flipped, low, high):
    @pl.loop(low, high)
    def _(n):
        g = lax.rem(n, d.groups)
        top = n // d.groups * d.step
        acc = [jnp.zeros((SUB, W), F32) for _ in range(d.step)]
        for b in range(TAPS):
            near = TAPS - 1 - b if flipped else b
            lines = [
                image[near, pl.ds(pl.multiple_of((top + t) * d.cl + g * SUB, SUB), SUB), :]
                for t in range(d.step + TAPS - 1)
            ]
            for a in range(TAPS):
                w = weights[a * TAPS + b, pl.ds(pl.multiple_of(g * SUB, SUB), SUB), :]
                down = TAPS - 1 - a if flipped else a
                acc = [acc[i] + w * lines[i + down] for i in range(d.step)]
        for i in range(d.step):
            out[pl.ds(pl.multiple_of((top + i) * d.cl + g * SUB, SUB), SUB), :] = acc[i]


def tap_tile(d, image, flat, acc, tile):
    base = tile * d.used
    for g in range(d.groups):
        mine = slice(g * SUB, (g + 1) * SUB)
        v = [flat[pl.ds(pl.multiple_of(base + i * d.cl + g * SUB, SUB), SUB), :] for i in range(d.tile)]
        for b in range(TAPS):
            lines = [
                image[b, pl.ds(pl.multiple_of(base + t * d.cl + g * SUB, SUB), SUB), :]
                for t in range(d.tile + TAPS - 1)
            ]
            for a in range(TAPS):
                part = v[0] * lines[a]
                for i in range(1, d.tile):
                    part = part + v[i] * lines[i + a]
                acc[a * TAPS + b, mine, :] = acc[a * TAPS + b, mine, :] + part


def tap_totals(d, acc, grad):
    lane = lane_iota()

    @pl.loop(0, d.groups)
    def _(g):
        at = pl.ds(pl.multiple_of(g * SUB, SUB), SUB)
        total = jnp.zeros((SUB, W), F32)
        for t in range(TAPS * TAPS):
            total = jnp.where(lane == t, jnp.sum(acc[t, at, :], axis=1, keepdims=True), total)
        grad[at, :] = total


def column_of(vector, out):
    for j in range(vector.shape[0]):
        n = vector.shape[1]
        line = jnp.broadcast_to(vector[j : j + 1, :], (W, n))
        out[j * n : (j + 1) * n, :] = jnp.transpose(line)


def first_peer(d, lon, offset):
    z = lax.rem(lon // d.core, d.zhi)
    mine = lon // (d.core * d.zhi) * d.core + lax.rem(lon, d.core)
    theirs = lax.rem(mine + offset, d.first)
    peer = (theirs // d.core * d.zhi + z) * d.core + lax.rem(theirs, d.core)
    return mine, theirs, peer


def second_peer(d, lon, offset):
    mine = lax.rem(lon // d.core, d.zhi)
    theirs = lax.rem(mine + offset, d.zhi)
    return mine, theirs, lon + (theirs - mine) * d.core


def share_copy(d, peers, count, offset, src, dst, send, recv, arriving=False):
    mine, theirs, peer = peers(d, lax.axis_index("lon"), offset)
    return pltpu.make_async_remote_copy(
        src_ref=src, dst_ref=dst.at[theirs if arriving else mine], send_sem=send.at[theirs],
        recv_sem=recv.at[theirs if arriving else mine], device_id={"lon": peer}, device_id_type=MESH,
    )


def share_start(d, peers, count, src, dst, send, recv):
    mine, _, _ = peers(d, lax.axis_index("lon"), 1)
    for s in range(1, count):
        share_copy(d, peers, count, s, src, dst, send, recv).start()
    dst[mine] = src[...]


def share_wait(d, peers, count, src, dst, send, recv):
    for s in range(1, count):
        share_copy(d, peers, count, s, src, dst, send, recv, True).wait_recv()
    for s in range(1, count):
        share_copy(d, peers, count, s, src, dst, send, recv).wait_send()


def gather_copy(d, offset, src, dst, send, recv, arriving=False):
    me = lax.axis_index("lev")
    peer = lev_peer(d, me, offset)
    return pltpu.make_async_remote_copy(
        src_ref=src, dst_ref=dst.at[peer if arriving else me], send_sem=send.at[peer],
        recv_sem=recv.at[peer if arriving else me], device_id={"lev": peer}, device_id_type=MESH,
    )


def block_kernel(d, snap_hbm, kern, cot_hbm, mask, gain, shift, w_in_hbm, w_out_hbm, result, out, grads,
                 rows, pad32, wide, tail, shifted, weights, image, fold, sums,
                 gains, shifts, normed, rstds, lifted, upstream, projected, d_lifted, blocks, w_in, w_out,
                 grad, part1, total1, part2, total2, gathered, gflat, snap, cot, d_active, products, move, padded, halo,
                 hs, hr, fs, fr, hs2, hr2, fs2, fr2, rs, rbuf, cs, cbuf, us, ubuf, ds, dbuf,
                 w_sem, e_send, e_recv, e2_send, e2_recv, r_send, r_recv, c_send, c_recv, u_send, u_recv, d_send, d_recv,
                 p1s, p1r, p2s, p2r, gs, gr):
    lev, lon = lax.axis_index("lev"), lax.axis_index("lon")
    barrier = pltpu.get_barrier_semaphore()
    greet(d, barrier)
    for s in range(1, d.first):
        signal(barrier, {"lon": first_peer(d, lon, s)[2]})
    for s in range(1, d.zhi):
        signal(barrier, {"lon": second_peer(d, lon, s)[2]})
    snap_copy = pltpu.make_async_copy(snap_hbm, snap, w_sem.at[2])
    snap_copy.start()
    cot_copy = pltpu.make_async_copy(cot_hbm, cot, w_sem.at[3])
    cot_copy.start()
    w_copies = [pltpu.make_async_copy(w_in_hbm, w_in, w_sem.at[0]), pltpu.make_async_copy(w_out_hbm, w_out, w_sem.at[1])]
    for copy in w_copies:
        copy.start()
    edge = (hs, hr, fs, fr, (e_send, e_recv))
    edge2 = (hs2, hr2, fs2, fr2, (e2_send, e2_recv))
    residual = (d, rs, rbuf, r_send, r_recv)
    forward = (d, cs, cbuf, c_send, c_recv)
    upward = (d, us, ubuf, u_send, u_recv)
    backward = (d, ds, dbuf, d_send, d_recv)

    with phase("prep"):
        snap_copy.wait()
        for c in range(d.cl):
            rows[pl.ds(c, d.rows, stride=d.cl), :] = snap[c].astype(F32)
        tail[...] = jnp.zeros_like(tail)
        fs[...] = jnp.zeros_like(fs)
        fs2[...] = jnp.zeros_like(fs2)
        pack_edges(d, rows, hs, fs, tail)
        for k in range(d.levs):
            rs[k] = rows[k * d.used : (k + 1) * d.used, :].astype(BF16)
    with phase("meet"):
        met(d, barrier, d.first - 1 + d.zhi - 1)
    edge_start(d, *edge)
    early = d.levs // 2
    blocks_start(*residual, 1, early)

    with phase("weights"):
        for j, m in enumerate(moves()):
            move[:, j * W : (j + 1) * W] = m
        wide[...] = jnp.zeros_like(wide)
        wide[: TAPS * TAPS, :] = kern[...].astype(F32)
        for j in range(0, d.channels, W):
            n = min(W, d.channels - j)
            gflat[j : j + n, :] = jnp.transpose(wide[:, j : j + n])
        mine = gflat[pl.ds(pl.multiple_of(lev * d.cl, SUB), d.cl), :]
        for t in range(TAPS * TAPS):
            weights[t] = jnp.broadcast_to(mine[:, t : t + 1], (d.cl, W))
        for b in range(TAPS):
            shifted[b, : REACH * d.cl, :] = jnp.zeros((REACH * d.cl, W), F32)
            image[b, : REACH * d.cl, :] = jnp.zeros((REACH * d.cl, W), F32)
            image[b, (REACH + d.rows) * d.cl :, :] = jnp.zeros((REACH * d.cl, W), F32)

    with phase("edge_wait"):
        edge_wait(d, *edge)
    with phase("shifts"):
        build_shifts(d, rows, hr, halo, padded, tail, move, shifted)
        fold_shifts(d, fr, padded, tail, move, shifted, (REACH + d.rows) * d.cl)

    with phase("conv"):
        sub = lax.broadcasted_iota(jnp.int32, (d.block - d.used, W), 0)

        @pl.loop(1, d.levs + 1)
        def _(s):
            peer = lev_peer(d, lev, s)
            convolve_tile(d, shifted, weights, peer, pad32, sub)
            cs[peer] = pad32[...].astype(BF16)

            @pl.when(s < d.levs)
            def _():
                block_copy(d, lev, s, cs, cbuf, c_send, c_recv).start()

        cbuf[lev] = cs[lev]

    chunk = 256
    chunks = [slice(n, n + chunk) for n in range(0, d.hidden, chunk)]
    with phase("upstream"):
        cot_copy.wait()
        column_of(gain[...], gains)
        column_of(shift[...], shifts)
        wet = mask[...].astype(F32)
        for r in range(d.tile):
            up = cot[r].astype(F32) * wet[r : r + 1, :]
            upstream[r * W : (r + 1) * W, :] = jnp.transpose(up).astype(BF16)
            for k in range(d.levs):
                blocks[k, r * d.cl : (r + 1) * d.cl, :] = up[k * d.cl : (k + 1) * d.cl]
        for k in range(d.levs):
            us[k] = blocks[k, : d.used, :].astype(BF16)
        for copy in w_copies:
            copy.wait()
        for f in chunks:
            d_active[:, f] = lax.dot_general(
                upstream[...], w_out[f, :], (((1,), (1,)), ((), ())), preferred_element_type=F32
            )
    with phase("conv_wait"):
        blocks_arrive(*forward)
    blocks_start(*residual, early)

    with phase("norm"):
        for k in range(d.levs):
            v = cbuf[k].astype(F32)
            for r in range(d.tile):
                at = d.used + 2 * r
                normed[r, k * d.cl : (k + 1) * d.cl, :] = v[r * d.cl : (r + 1) * d.cl] + (v[at : at + 1] + v[at + 1 : at + 2])
        inv = 1.0 / d.channels
        for r in range(d.tile):
            v = normed[r]
            v = v - jnp.sum(v, axis=0, keepdims=True) * inv
            spread = jnp.sum(v * v, axis=0, keepdims=True) * inv
            rstd = lax.rsqrt(spread + epsilon)
            v = v * rstd
            normed[r] = v
            rstds[r : r + 1, :] = rstd
            lifted[r * W : (r + 1) * W, :] = jnp.transpose(v * gains[...] + shifts[...]).astype(BF16)

    with phase("mlp"):
        for n, f in enumerate(chunks):
            hidden = jnp.dot(lifted[...], w_in[:, f], preferred_element_type=F32)
            share = 0.5 * (1.0 + lax.erf(hidden * root_half))
            active = (hidden * share).astype(BF16)
            slope = share + hidden * jnp.exp(-0.5 * hidden * hidden) * inv_root_tau
            d_hidden = (d_active[:, f] * slope).astype(BF16)
            p = jnp.dot(active, w_out[f, :], preferred_element_type=F32)
            q = lax.dot_general(w_in[:, f], d_hidden, (((1,), (1,)), ((), ())), preferred_element_type=F32)
            if n == 0:
                projected[...] = p
                d_lifted[...] = q
            else:
                projected[...] += p
                d_lifted[...] += q

    with phase("dconv"):
        for r in range(d.tile):
            dn = d_lifted[:, r * W : (r + 1) * W] * gains[...]
            v = normed[r]
            mean = jnp.sum(dn, axis=0, keepdims=True) * inv
            along = jnp.sum(dn * v, axis=0, keepdims=True) * inv
            normed[r] = rstds[r : r + 1, :] * (dn - mean - v * along)
            for k in range(d.levs):
                blocks[k, r * d.cl : (r + 1) * d.cl, :] = normed[r, k * d.cl : (k + 1) * d.cl, :]
        for k in range(d.levs):
            ds[k] = blocks[k, : d.used, :].astype(BF16)
    blocks_start(*backward)

    blocks_start(*upward)
    products[...] = jnp.zeros_like(products)
    with phase("grad"):

        @pl.loop(0, d.levs)
        def _(s):
            tile = lev_peer(d, lev, d.levs - s)

            @pl.when(s > 0)
            def _():
                block_copy(d, lev, d.levs - s, ds, dbuf, d_send, d_recv, True).wait_recv()

            rows[pl.ds(pl.multiple_of(tile * d.used, SUB), d.used), :] = dbuf[tile].astype(F32)
            tap_tile(d, shifted, rows, products, tile)

    with phase("pack2"):
        pack_edges(d, rows, hs2, fs2, tail)
    edge_start(d, *edge2)
    tap_totals(d, products, grad)
    first = (d, first_peer, d.first, grad, part1, p1s, p1r)
    share_start(*first)

    with phase("result"):
        blocks_arrive(*residual)
        for k in range(d.levs):
            blocks[k, : d.used, :] = rbuf[k].astype(F32)
        for r in range(d.tile):
            moved = jnp.transpose(projected[r * W : (r + 1) * W, :])
            for k in range(d.levs):
                part = slice(k * d.cl, (k + 1) * d.cl)
                shifts[part, :] = wet[r : r + 1, :] * (blocks[k, r * d.cl : (r + 1) * d.cl, :] + moved[part])
            result[r] = shifts[...].astype(BF16)

    with phase("share1_wait"):
        share_wait(*first)
    total1[...] = sum(part1[i] for i in range(d.first))
    second = (d, second_peer, d.zhi, total1, part2, p2s, p2r)
    share_start(*second)

    with phase("edge2_wait"):
        edge_wait(d, *edge2)
    with phase("shifts2"):
        build_shifts(d, rows, hr2, halo, padded, tail, move, image)
        fold_shifts(d, fr2, padded, tail, move, fold, 0)

    with phase("adjoint"):
        steps = d.rows // d.step * d.groups
        half = steps // 2
        correlate(d, image, weights, sums, True, 0, half)

    with phase("share2_wait"):
        share_wait(*second)
    total2[...] = sum(part2[i] for i in range(d.zhi))
    for s in range(1, d.levs):
        gather_copy(d, s, total2, gathered, gs, gr).start()
    gathered[lev] = total2[...]

    with phase("adjoint2"):
        correlate(d, image, weights, sums, True, half, steps)
    with phase("edge_term"):
        for m in range(REACH):
            for g in range(d.groups):
                at = (d.rows - 1 - m) * d.cl + g * SUB
                acc = sums[at : at + SUB, :]
                for k in range(REACH - m):
                    for b in range(TAPS):
                        w = weights[(REACH + 1 + m + k) * TAPS + b, g * SUB : (g + 1) * SUB, :]
                        acc = acc + w * fold[b, k * d.cl + g * SUB : k * d.cl + (g + 1) * SUB, :]
                sums[at : at + SUB, :] = acc
    with phase("u_wait"):
        blocks_arrive(*upward)
    with phase("finish"):
        for k in range(d.levs):
            part = slice(k * d.used, (k + 1) * d.used)
            sums[part, :] = sums[part, :] + ubuf[k].astype(F32)
        for c in range(d.cl):
            out[c] = sums[pl.ds(c, d.rows, stride=d.cl), :].astype(BF16)

    with phase("gather_wait"):
        for s in range(1, d.levs):
            gather_copy(d, s, total2, gathered, gs, gr, True).wait_recv()
    for k in range(d.levs):
        gflat[k * d.cl : (k + 1) * d.cl, :] = gathered[k]
    for j in range(0, d.channels, W):
        n = min(W, d.channels - j)
        grads[:, j : j + n] = jnp.transpose(gflat[j : j + n, :])[: TAPS * TAPS]
    for s in range(1, d.levs):
        gather_copy(d, s, total2, gathered, gs, gr).wait_send()
    blocks_sent(*residual)
    blocks_sent(*forward)
    blocks_sent(*upward)
    blocks_sent(*backward)


def settle(*refs):
    for source, target in zip(refs[:3], refs[3:]):
        target[...] = source[...]


VMEM = pl.BlockSpec(memory_space=pltpu.VMEM)
ANY = pl.BlockSpec(memory_space=pl.ANY)
DMA = pltpu.SemaphoreType.DMA
LIMIT = 60 * 1024 * 1024


def shards(snapshot, cotangent, ocean_mask, kernel, norm_gain, norm_shift, weight_in, weight_out):
    levs, lons = lax.axis_size("lev"), lax.axis_size("lon")
    cl, rows, _ = snapshot.shape
    d = Dims(levs, lons, cl * levs, rows, weight_in.shape[1])
    sds = jax.ShapeDtypeStruct
    f32 = lambda *shape: pltpu.VMEM(shape, F32)
    b16 = lambda *shape: pltpu.VMEM(shape, BF16)
    flat = (d.rows * d.cl, W)
    image = (TAPS, (d.rows + 2 * REACH) * d.cl, W)
    halo = (-(-max(d.packs, REACH) * d.cl // 16) * 16, W)
    north = (-(-REACH * d.cl // 16) * 16, W)
    cells = d.tile * W
    share = (d.cl, W)
    result, d_snapshot, grads = pl.pallas_call(
        functools.partial(block_kernel, d),
        name="block",
        out_shape=(
            sds((d.tile, d.channels, W), BF16), sds((d.cl, d.rows, W), BF16), sds((TAPS * TAPS, d.channels), F32),
        ),
        in_specs=[ANY, VMEM, ANY, VMEM, VMEM, VMEM, ANY, ANY],
        out_specs=(VMEM,) * 3,
        scratch_shapes=[
            f32(*flat), f32(d.block, W), f32(W, d.channels), f32(*halo), f32(*image), f32(TAPS * TAPS, d.cl, W),
            f32(*image), f32(TAPS, REACH * d.cl, W), f32(*flat),
            f32(d.channels, W), f32(d.channels, W), f32(d.tile, d.channels, W), f32(d.tile, W),
            b16(cells, d.channels), b16(cells, d.channels), f32(cells, d.channels), f32(d.channels, cells),
            f32(d.levs, d.block, W), b16(*weight_in.shape), b16(*weight_out.shape),
            f32(*share), f32(d.first, *share), f32(*share), f32(d.zhi, *share), f32(*share),
            f32(d.levs, *share), f32(d.channels, W), b16(d.cl, d.rows, W), b16(d.tile, d.channels, W),
            f32(cells, d.hidden), f32(TAPS * TAPS, d.cl, W),
            b16(2 * W, 6 * W), b16(max(d.rows * d.cl // 3, REACH * d.cl), 2 * W), f32(*flat),
            *[b16(*halo), b16(2, *halo), b16(*north), b16(3, *north)] * 2,
            b16(d.levs, d.used, W), b16(d.levs, d.used, W), b16(d.levs, d.block, W), b16(d.levs, d.block, W),
            *[b16(d.levs, d.used, W)] * 4,
            DMA((4,)), *[DMA((5,))] * 4, *[DMA((d.levs,))] * 8,
            DMA((d.first,)), DMA((d.first,)), DMA((d.zhi,)), DMA((d.zhi,)), DMA((d.levs,)), DMA((d.levs,)),
        ],
        compiler_params=pltpu.CompilerParams(collective_id=0, has_side_effects=True, vmem_limit_bytes=LIMIT),
    )(
        snapshot, kernel.T, jnp.swapaxes(cotangent, 0, 1), ocean_mask,
        norm_gain.reshape(-1, min(W, d.channels)), norm_shift.reshape(-1, min(W, d.channels)), weight_in, weight_out,
    )
    result, d_snapshot, grads = pl.pallas_call(
        settle,
        name="settle",
        out_shape=tuple(sds(x.shape, x.dtype) for x in (result, d_snapshot, grads)),
        in_specs=[VMEM] * 3,
        out_specs=(VMEM,) * 3,
    )(result, d_snapshot, grads)
    return jnp.swapaxes(result, 0, 1), d_snapshot, grads.T


def solution(mesh):
    placed = (
        P("lev", None, "lon"),
        P(None, "lev", "lon"),
        P("lev", "lon"),
        P(),
        P(),
        P(),
        P(),
        P(),
    )
    return jax.shard_map(
        shards,
        mesh=mesh,
        in_specs=placed,
        out_specs=(P(None, "lev", "lon"), P("lev", None, "lon"), P()),
        check_vma=False,
    )
```

```python
import contextlib
import functools

import jax
import jax.numpy as jnp
from jax import lax
from jax.experimental import pallas as pl
from jax.experimental.pallas import tpu as pltpu
from jax.sharding import PartitionSpec as P

MESH = pl.DeviceIdType.MESH
F32 = jnp.float32
BF16 = jnp.bfloat16
TAPS = 7
REACH = 3
W = 128
SUB = 8

epsilon = 1e-06
root_half = 0.7071067811865476
inv_root_tau = 0.3989422804014327


TRACE = False


def phase(name):
    return jax.named_scope(name) if TRACE else contextlib.nullcontext()


class Dims:
    def __init__(self, levs, lons, channels, rows, hidden):
        self.levs, self.lons, self.channels, self.rows, self.hidden = levs, lons, channels, rows, hidden
        self.cl = channels // levs
        self.tile = rows // levs
        self.room = -(-(self.cl + 2) // 8) * 8
        self.quad = 4
        self.used = self.tile * self.cl
        self.groups = self.cl // SUB
        self.step = max(r for r in (8, 6, 4, 3) if rows % r == 0)
        self.packs = -(-rows // 16)
        self.core = 2
        self.zhi = 4 if lons == 32 else 2
        self.x = lons // (self.core * self.zhi)
        self.first = self.x * self.core


def lane_iota(shape=(SUB, W)):
    return lax.broadcasted_iota(jnp.int32, shape, 1)


def lev_peer(d, me, offset):
    return lax.rem(me + offset, d.levs)


def lon_targets(d):
    me = lax.axis_index("lon")
    n = d.lons
    mirror = n - 1 - me
    right, left = lax.rem(me + 1, n), lax.rem(me + n - 1, n)
    return me, (right, left), (mirror, lax.rem(mirror + 1, n), lax.rem(mirror + n - 1, n))


def signal(sem, where):
    pl.semaphore_signal(sem, inc=1, device_id=where, device_id_type=MESH)


def greet(d, sem):
    lev = lax.axis_index("lev")
    me, sides, mirrors = lon_targets(d)

    @pl.loop(1, d.levs)
    def _(s):
        signal(sem, {"lev": lev_peer(d, lev, s)})

    for side in sides:
        signal(sem, {"lon": side})
    for mirror in mirrors:

        @pl.when(mirror != me)
        def _(mirror=mirror):
            signal(sem, {"lon": mirror})


def met(d, sem, more=0):
    me, _, mirrors = lon_targets(d)
    own = sum(jnp.where(mirror == me, 1, 0) for mirror in mirrors)
    pl.semaphore_wait(sem, d.levs - 1 + 2 + len(mirrors) + more - own)


def edge_copies(d, hs, hr, fs, fr, sems):
    me, sides, mirrors = lon_targets(d)
    send, recv = sems
    for j, side in enumerate(sides):
        yield None, pltpu.make_async_remote_copy(
            src_ref=hs, dst_ref=hr.at[j], send_sem=send.at[j], recv_sem=recv.at[j],
            device_id={"lon": side}, device_id_type=MESH,
        ), None
    for j, mirror in enumerate(mirrors):
        yield mirror != me, pltpu.make_async_remote_copy(
            src_ref=fs, dst_ref=fr.at[j], send_sem=send.at[2 + j], recv_sem=recv.at[2 + j],
            device_id={"lon": mirror}, device_id_type=MESH,
        ), pltpu.make_async_copy(fs, fr.at[j], recv.at[2 + j])


def edge_start(d, *refs):
    for away, remote, own in edge_copies(d, *refs):
        if away is None:
            remote.start()
        else:
            pl.when(away)(remote.start)
            pl.when(jnp.logical_not(away))(own.start)


def edge_wait(d, *refs):
    for away, remote, own in edge_copies(d, *refs):
        if away is None:
            remote.wait()
        else:
            pl.when(away)(remote.wait)
            pl.when(jnp.logical_not(away))(own.wait)


def block_copy(d, me, offset, src, dst, send, recv, arriving=False):
    peer = lev_peer(d, me, offset)
    return pltpu.make_async_remote_copy(
        src_ref=src.at[peer],
        dst_ref=dst.at[peer if arriving else me],
        send_sem=send.at[peer],
        recv_sem=recv.at[peer if arriving else me],
        device_id={"lev": peer},
        device_id_type=MESH,
    )


def blocks_start(d, src, dst, send, recv, low=1, high=None):
    me = lax.axis_index("lev")

    @pl.loop(low, high or d.levs)
    def _(s):
        block_copy(d, me, s, src, dst, send, recv).start()

    if low == 1:
        dst[me] = src[me]


def blocks_arrive(d, src, dst, send, recv):
    me = lax.axis_index("lev")

    @pl.loop(1, d.levs)
    def _(s):
        block_copy(d, me, s, src, dst, send, recv, True).wait_recv()


def blocks_sent(d, src, dst, send, recv):
    me = lax.axis_index("lev")

    @pl.loop(1, d.levs)
    def _(s):
        block_copy(d, me, s, src, dst, send, recv).wait_send()


def pack_edges(d, rows, hs, fs, tail):
    slot = lane_iota() >> 3

    @pl.loop(0, d.groups)
    def _(g):
        for q in range(d.packs):
            both = jnp.zeros((SUB, W), F32)
            for r in range(16 * q, min(16 * q + 16, d.rows)):
                s = r - 16 * q
                v = rows[pl.ds(pl.multiple_of(r * d.cl + g * SUB, SUB), SUB), :]
                both = jnp.where(slot == s, pltpu.roll(v, (8 * s - (W - REACH)) % W, 1), both)
            tail[pl.ds(pl.multiple_of(q * d.cl + g * SUB, SUB), SUB), :] = both

    hs[...] = tail[...].astype(BF16)
    north = (d.rows - REACH) * d.cl
    fs[: REACH * d.cl, :] = rows[north : north + REACH * d.cl, :].astype(BF16)


def pack_tile(d, rows, tail, tile):
    slot = lane_iota() >> 3
    for i in range(d.tile):
        r = tile * d.tile + i
        s = lax.rem(r, 16)
        turn = lax.rem(8 * s + REACH, W)
        for g in range(d.groups):
            v = rows[pl.ds(pl.multiple_of(r * d.cl + g * SUB, SUB), SUB), :]
            at = pl.ds(pl.multiple_of(r // 16 * d.cl + g * SUB, SUB), SUB)
            tail[at, :] = jnp.where(slot == s, pltpu.roll(v, turn, 1), tail[at, :])


def moves():
    row = lax.broadcasted_iota(jnp.int32, (2 * W, W), 0)
    column = lax.broadcasted_iota(jnp.int32, (2 * W, W), 1)
    for b in (0, 1, 2, 4, 5, 6):
        source = column + (b - REACH)
        yield jnp.where(row == jnp.where(source < 0, source + 2 * W, source), 1.0, 0.0).astype(BF16)


def build_shifts(d, rows, hr, halo, padded, both, move, out):
    west = (lax.broadcasted_iota(jnp.int32, both.shape, 1) & 7) < REACH
    both[...] = jnp.where(west, hr[0].astype(F32), hr[1].astype(F32))

    @pl.loop(0, d.groups)
    def _(g):
        for r in range(d.rows):
            q, s = divmod(r, 16)
            v = both[pl.ds(pl.multiple_of(q * d.cl + g * SUB, SUB), SUB), :]
            to = pl.ds(pl.multiple_of(r * d.cl + g * SUB, SUB), SUB)
            halo[to, :] = pltpu.roll(v, (W - REACH - 8 * s) % W, 1)

    count = d.rows * d.cl
    step = count // 3

    @pl.loop(0, 3)
    def _(n):
        here = pl.ds(pl.multiple_of(n * step, SUB), step)
        to = pl.ds(pl.multiple_of(REACH * d.cl + n * step, SUB), step)
        x = rows[here, :]
        out[REACH, to, :] = x
        padded[:step, :W] = x.astype(BF16)
        padded[:step, W:] = halo[here, :].astype(BF16)
        for j in range(3):
            moved = jnp.dot(padded[:step, :], move[:, 2 * j * W : 2 * (j + 1) * W], preferred_element_type=F32)
            for i in range(2):
                b = (0, 1, 2, 4, 5, 6)[2 * j + i]
                out[b, to, :] = moved[:, i * W : (i + 1) * W]


def fold_shifts(d, fr, padded, both, move, out, base):
    count = REACH * d.cl
    flip = lax.broadcasted_iota(jnp.int32, (W, W), 0) + lax.broadcasted_iota(jnp.int32, (W, W), 1) == W - 1
    flip = flip.astype(F32).astype(BF16)
    centre, left, right = (jnp.dot(fr[j], flip, preferred_element_type=F32) for j in range(3))
    low = lax.broadcasted_iota(jnp.int32, (d.cl, W), 1) < W // 2
    for m in range(REACH):
        src = slice((REACH - 1 - m) * d.cl, (REACH - m) * d.cl)
        out[REACH, base + m * d.cl : base + (m + 1) * d.cl, :] = centre[src]
        both[m * d.cl : (m + 1) * d.cl, :] = jnp.where(low, right[src], left[src])
    padded[:count, :W] = out[REACH, base : base + count, :].astype(BF16)
    padded[:count, W:] = both[:count, :].astype(BF16)
    for j in range(3):
        moved = jnp.dot(padded[:count, :], move[:, 2 * j * W : 2 * (j + 1) * W], preferred_element_type=F32)
        for i in range(2):
            b = (0, 1, 2, 4, 5, 6)[2 * j + i]
            out[b, base : base + count, :] = moved[:, i * W : (i + 1) * W]


def convolve_rows(d, image, weights, r, first, pad32, sub):
    base = (first * d.tile + r) * d.cl
    for g in range(d.groups):
        acc = [jnp.zeros((SUB, W), F32) for _ in range(d.quad)]
        for b in range(TAPS):
            lines = [
                image[b, pl.ds(pl.multiple_of(base + t * d.cl + g * SUB, SUB), SUB), :]
                for t in range((d.quad - 1) * d.tile + TAPS)
            ]
            for a in range(TAPS):
                w = weights[a * TAPS + b, g * SUB : (g + 1) * SUB, :]
                acc = [acc[k] + w * lines[k * d.tile + a] for k in range(d.quad)]
        for k in range(d.quad):
            pad32[k, g * SUB : (g + 1) * SUB, :] = acc[k]
    for k in range(d.quad):
        v = pad32[k, : d.cl, :]
        mean = jnp.sum(v, axis=0, keepdims=True) * (1.0 / d.cl)
        high = mean.astype(BF16).astype(F32)
        low = (mean - high).astype(BF16).astype(F32)
        pad32[k, : d.cl, :] = v - (high + low)
        pad32[k, d.cl :, :] = jnp.where(sub == 0, high, jnp.where(sub == 1, low, 0.0))


def row_copy(d, me, peer, r, src, dst, send, recv, arriving=False):
    return pltpu.make_async_remote_copy(
        src_ref=src.at[r, peer],
        dst_ref=dst.at[r, peer if arriving else me],
        send_sem=send.at[r, peer],
        recv_sem=recv.at[r, peer if arriving else me],
        device_id={"lev": peer},
        device_id_type=MESH,
    )


def rows_arrive(d, r, *refs):
    me = lax.axis_index("lev")

    @pl.loop(1, d.levs)
    def _(s):
        row_copy(d, me, lev_peer(d, me, s), r, *refs, True).wait_recv()


def rows_sent(d, *refs):
    me = lax.axis_index("lev")
    for r in range(d.tile):

        @pl.loop(1, d.levs)
        def _(s):
            row_copy(d, me, lev_peer(d, me, s), r, *refs).wait_send()


def correlate(d, image, weights, out, flipped, low, high):
    @pl.loop(low, high)
    def _(n):
        g = lax.rem(n, d.groups)
        top = n // d.groups * d.step
        acc = [jnp.zeros((SUB, W), F32) for _ in range(d.step)]
        for b in range(TAPS):
            near = TAPS - 1 - b if flipped else b
            lines = [
                image[near, pl.ds(pl.multiple_of((top + t) * d.cl + g * SUB, SUB), SUB), :]
                for t in range(d.step + TAPS - 1)
            ]
            for a in range(TAPS):
                w = weights[a * TAPS + b, pl.ds(pl.multiple_of(g * SUB, SUB), SUB), :]
                down = TAPS - 1 - a if flipped else a
                acc = [acc[i] + w * lines[i + down] for i in range(d.step)]
        for i in range(d.step):
            out[pl.ds(pl.multiple_of((top + i) * d.cl + g * SUB, SUB), SUB), :] = acc[i]


def tap_tile(d, image, flat, acc, tile):
    base = tile * d.used
    for g in range(d.groups):
        mine = slice(g * SUB, (g + 1) * SUB)
        v = [flat[pl.ds(pl.multiple_of(base + i * d.cl + g * SUB, SUB), SUB), :] for i in range(d.tile)]
        for b in range(TAPS):
            lines = [
                image[b, pl.ds(pl.multiple_of(base + t * d.cl + g * SUB, SUB), SUB), :]
                for t in range(d.tile + TAPS - 1)
            ]
            for a in range(TAPS):
                part = v[0] * lines[a]
                for i in range(1, d.tile):
                    part = part + v[i] * lines[i + a]
                acc[a * TAPS + b, mine, :] = acc[a * TAPS + b, mine, :] + part


def tap_totals(d, acc, grad):
    lane = lane_iota()

    @pl.loop(0, d.groups)
    def _(g):
        at = pl.ds(pl.multiple_of(g * SUB, SUB), SUB)
        total = jnp.zeros((SUB, W), F32)
        for t in range(TAPS * TAPS):
            total = jnp.where(lane == t, jnp.sum(acc[t, at, :], axis=1, keepdims=True), total)
        grad[at, :] = total


def column_of(vector, out):
    for j in range(vector.shape[0]):
        n = vector.shape[1]
        line = jnp.broadcast_to(vector[j : j + 1, :], (W, n))
        out[j * n : (j + 1) * n, :] = jnp.transpose(line)


def first_peer(d, lon, offset):
    z = lax.rem(lon // d.core, d.zhi)
    mine = lon // (d.core * d.zhi) * d.core + lax.rem(lon, d.core)
    theirs = lax.rem(mine + offset, d.first)
    peer = (theirs // d.core * d.zhi + z) * d.core + lax.rem(theirs, d.core)
    return mine, theirs, peer


def second_peer(d, lon, offset):
    mine = lax.rem(lon // d.core, d.zhi)
    theirs = lax.rem(mine + offset, d.zhi)
    return mine, theirs, lon + (theirs - mine) * d.core


def share_copy(d, peers, count, offset, src, dst, send, recv, arriving=False):
    mine, theirs, peer = peers(d, lax.axis_index("lon"), offset)
    return pltpu.make_async_remote_copy(
        src_ref=src, dst_ref=dst.at[theirs if arriving else mine], send_sem=send.at[theirs],
        recv_sem=recv.at[theirs if arriving else mine], device_id={"lon": peer}, device_id_type=MESH,
    )


def share_start(d, peers, count, src, dst, send, recv):
    mine, _, _ = peers(d, lax.axis_index("lon"), 1)
    for s in range(1, count):
        share_copy(d, peers, count, s, src, dst, send, recv).start()
    dst[mine] = src[...]


def share_wait(d, peers, count, src, dst, send, recv):
    for s in range(1, count):
        share_copy(d, peers, count, s, src, dst, send, recv, True).wait_recv()
    for s in range(1, count):
        share_copy(d, peers, count, s, src, dst, send, recv).wait_send()


def gather_copy(d, offset, src, dst, send, recv, arriving=False):
    me = lax.axis_index("lev")
    peer = lev_peer(d, me, offset)
    return pltpu.make_async_remote_copy(
        src_ref=src, dst_ref=dst.at[peer if arriving else me], send_sem=send.at[peer],
        recv_sem=recv.at[peer if arriving else me], device_id={"lev": peer}, device_id_type=MESH,
    )


def block_kernel(d, snap_hbm, kern, cot_hbm, mask, gain, shift, w_in_hbm, w_out_hbm, result, out, grads,
                 rows, pad32, wide, tail, shifted, weights, image, fold, sums,
                 gains, shifts, normed, rstds, lifted, upstream, projected, d_lifted, blocks, w_in, w_out,
                 grad, part1, total1, part2, total2, gathered, gflat, snap, cot, d_active, products, move, padded, halo,
                 hs, hr, fs, fr, hs2, hr2, fs2, fr2, rs, rbuf, cs, cbuf, us, ubuf, ds, dbuf,
                 w_sem, e_send, e_recv, e2_send, e2_recv, r_send, r_recv, c_send, c_recv, u_send, u_recv, d_send, d_recv,
                 p1s, p1r, p2s, p2r, gs, gr):
    lev, lon = lax.axis_index("lev"), lax.axis_index("lon")
    barrier = pltpu.get_barrier_semaphore()
    greet(d, barrier)
    for s in range(1, d.first):
        signal(barrier, {"lon": first_peer(d, lon, s)[2]})
    for s in range(1, d.zhi):
        signal(barrier, {"lon": second_peer(d, lon, s)[2]})
    snap_copy = pltpu.make_async_copy(snap_hbm, snap, w_sem.at[2])
    snap_copy.start()
    cot_copy = pltpu.make_async_copy(cot_hbm, cot, w_sem.at[3])
    cot_copy.start()
    w_copies = [pltpu.make_async_copy(w_in_hbm, w_in, w_sem.at[0]), pltpu.make_async_copy(w_out_hbm, w_out, w_sem.at[1])]
    for copy in w_copies:
        copy.start()
    edge = (hs, hr, fs, fr, (e_send, e_recv))
    edge2 = (hs2, hr2, fs2, fr2, (e2_send, e2_recv))
    residual = (d, rs, rbuf, r_send, r_recv)
    forward = (cs, cbuf, c_send, c_recv)
    upward = (d, us, ubuf, u_send, u_recv)
    backward = (ds, dbuf, d_send, d_recv)

    with phase("prep"):
        snap_copy.wait()
        for c in range(d.cl):
            rows[pl.ds(c, d.rows, stride=d.cl), :] = snap[c].astype(F32)
        tail[...] = jnp.zeros_like(tail)
        fs[...] = jnp.zeros_like(fs)
        fs2[...] = jnp.zeros_like(fs2)
        pack_edges(d, rows, hs, fs, tail)
        for k in range(d.levs):
            rs[k] = rows[k * d.used : (k + 1) * d.used, :].astype(BF16)
    with phase("meet"):
        met(d, barrier, d.first - 1 + d.zhi - 1)
    edge_start(d, *edge)
    blocks_start(*residual)

    with phase("weights"):
        for j, m in enumerate(moves()):
            move[:, j * W : (j + 1) * W] = m
        wide[...] = jnp.zeros_like(wide)
        wide[: TAPS * TAPS, :] = kern[...].astype(F32)
        for j in range(0, d.channels, W):
            n = min(W, d.channels - j)
            gflat[j : j + n, :] = jnp.transpose(wide[:, j : j + n])
        mine = gflat[pl.ds(pl.multiple_of(lev * d.cl, SUB), d.cl), :]
        for t in range(TAPS * TAPS):
            weights[t] = jnp.broadcast_to(mine[:, t : t + 1], (d.cl, W))
        for b in range(TAPS):
            shifted[b, : REACH * d.cl, :] = jnp.zeros((REACH * d.cl, W), F32)
            image[b, : REACH * d.cl, :] = jnp.zeros((REACH * d.cl, W), F32)
            image[b, (REACH + d.rows) * d.cl :, :] = jnp.zeros((REACH * d.cl, W), F32)

    with phase("edge_wait"):
        edge_wait(d, *edge)
    with phase("shifts"):
        build_shifts(d, rows, hr, halo, padded, tail, move, shifted)
        fold_shifts(d, fr, padded, tail, move, shifted, (REACH + d.rows) * d.cl)

    with phase("conv"):
        sub = lax.broadcasted_iota(jnp.int32, (d.room - d.cl, W), 0)
        parts = d.levs // d.quad

        @pl.loop(0, d.tile * parts)
        def _(n):
            r = n // parts
            tile = lax.rem(lev // d.quad + n, parts) * d.quad
            convolve_rows(d, shifted, weights, r, tile, pad32, sub)
            for k in range(d.quad):
                cs[r, tile + k] = pad32[k].astype(BF16)

                @pl.when(tile + k != lev)
                def _():
                    row_copy(d, lev, tile + k, r, *forward).start()

        for r in range(d.tile):
            cbuf[r, lev] = cs[r, lev]

    chunk = 256
    chunks = [slice(n, n + chunk) for n in range(0, d.hidden, chunk)]
    with phase("upstream"):
        cot_copy.wait()
        column_of(gain[...], gains)
        column_of(shift[...], shifts)
        wet = mask[...].astype(F32)
        for r in range(d.tile):
            up = cot[r].astype(F32) * wet[r : r + 1, :]
            upstream[r * W : (r + 1) * W, :] = jnp.transpose(up).astype(BF16)
            for k in range(d.levs):
                blocks[k, r * d.cl : (r + 1) * d.cl, :] = up[k * d.cl : (k + 1) * d.cl]
        for k in range(d.levs):
            us[k] = blocks[k].astype(BF16)
        for copy in w_copies:
            copy.wait()
        for f in chunks:
            d_active[:, f] = lax.dot_general(
                upstream[...], w_out[f, :], (((1,), (1,)), ((), ())), preferred_element_type=F32
            )
    inv = 1.0 / d.channels
    for r in range(d.tile):
        cells = slice(r * W, (r + 1) * W)
        with phase("conv_wait"):
            rows_arrive(d, r, *forward)
        with phase("norm"):
            for k in range(d.levs):
                v = cbuf[r, k].astype(F32)
                normed[r, k * d.cl : (k + 1) * d.cl, :] = v[: d.cl] + (v[d.cl : d.cl + 1] + v[d.cl + 1 : d.cl + 2])
            v = normed[r]
            v = v - jnp.sum(v, axis=0, keepdims=True) * inv
            spread = jnp.sum(v * v, axis=0, keepdims=True) * inv
            rstd = lax.rsqrt(spread + epsilon)
            v = v * rstd
            normed[r] = v
            rstds[r : r + 1, :] = rstd
            lifted[cells, :] = jnp.transpose(v * gains[...] + shifts[...]).astype(BF16)
        with phase("mlp"):
            for n, f in enumerate(chunks):
                hidden = jnp.dot(lifted[cells, :], w_in[:, f], preferred_element_type=F32)
                share = 0.5 * (1.0 + lax.erf(hidden * root_half))
                active = (hidden * share).astype(BF16)
                slope = share + hidden * jnp.exp(-0.5 * hidden * hidden) * inv_root_tau
                d_hidden = (d_active[cells, f] * slope).astype(BF16)
                p = jnp.dot(active, w_out[f, :], preferred_element_type=F32)
                q = lax.dot_general(w_in[:, f], d_hidden, (((1,), (1,)), ((), ())), preferred_element_type=F32)
                if n == 0:
                    projected[cells, :] = p
                    d_lifted[:, cells] = q
                else:
                    projected[cells, :] += p
                    d_lifted[:, cells] += q
        with phase("dconv"):
            dn = d_lifted[:, cells] * gains[...]
            v = normed[r]
            mean = jnp.sum(dn, axis=0, keepdims=True) * inv
            along = jnp.sum(dn * v, axis=0, keepdims=True) * inv
            normed[r] = rstds[r : r + 1, :] * (dn - mean - v * along)
            for k in range(d.levs):
                ds[r, k] = normed[r, k * d.cl : (k + 1) * d.cl, :].astype(BF16)

        @pl.loop(1, d.levs)
        def _(s):
            row_copy(d, lev, lev_peer(d, lev, s), r, *backward).start()

        dbuf[r, lev] = ds[r, lev]

    blocks_start(*upward)
    products[...] = jnp.zeros_like(products)
    with phase("grad"):

        @pl.loop(0, d.levs)
        def _(s):
            tile = lev_peer(d, lev, d.levs - s)

            @pl.when(s > 0)
            def _():
                for r in range(d.tile):
                    row_copy(d, lev, tile, r, *backward, True).wait_recv()

            for r in range(d.tile):
                at = pl.ds(pl.multiple_of(tile * d.used + r * d.cl, SUB), d.cl)
                rows[at, :] = dbuf[r, tile].astype(F32)
            tap_tile(d, shifted, rows, products, tile)
            pack_tile(d, rows, tail, tile)

    with phase("pack2"):
        hs2[...] = tail[...].astype(BF16)
        north = (d.rows - REACH) * d.cl
        fs2[: REACH * d.cl, :] = rows[north : north + REACH * d.cl, :].astype(BF16)
    edge_start(d, *edge2)
    tap_totals(d, products, grad)
    first = (d, first_peer, d.first, grad, part1, p1s, p1r)
    share_start(*first)

    with phase("result"):
        blocks_arrive(*residual)
        for k in range(d.levs):
            blocks[k] = rbuf[k].astype(F32)
        for r in range(d.tile):
            moved = jnp.transpose(projected[r * W : (r + 1) * W, :])
            for k in range(d.levs):
                part = slice(k * d.cl, (k + 1) * d.cl)
                shifts[part, :] = wet[r : r + 1, :] * (blocks[k, r * d.cl : (r + 1) * d.cl, :] + moved[part])
            result[r] = shifts[...].astype(BF16)

    with phase("share1_wait"):
        share_wait(*first)
    total1[...] = sum(part1[i] for i in range(d.first))
    second = (d, second_peer, d.zhi, total1, part2, p2s, p2r)
    share_start(*second)

    with phase("edge2_wait"):
        edge_wait(d, *edge2)
    with phase("shifts2"):
        build_shifts(d, rows, hr2, halo, padded, tail, move, image)
        fold_shifts(d, fr2, padded, tail, move, fold, 0)

    with phase("adjoint"):
        steps = d.rows // d.step * d.groups
        half = steps // 2
        correlate(d, image, weights, sums, True, 0, half)

    with phase("share2_wait"):
        share_wait(*second)
    total2[...] = sum(part2[i] for i in range(d.zhi))
    for s in range(1, d.levs):
        gather_copy(d, s, total2, gathered, gs, gr).start()
    gathered[lev] = total2[...]

    with phase("adjoint2"):
        correlate(d, image, weights, sums, True, half, steps)
    with phase("edge_term"):
        for m in range(REACH):
            for g in range(d.groups):
                at = (d.rows - 1 - m) * d.cl + g * SUB
                acc = sums[at : at + SUB, :]
                for k in range(REACH - m):
                    for b in range(TAPS):
                        w = weights[(REACH + 1 + m + k) * TAPS + b, g * SUB : (g + 1) * SUB, :]
                        acc = acc + w * fold[b, k * d.cl + g * SUB : k * d.cl + (g + 1) * SUB, :]
                sums[at : at + SUB, :] = acc
    with phase("u_wait"):
        blocks_arrive(*upward)
    with phase("finish"):
        for k in range(d.levs):
            part = slice(k * d.used, (k + 1) * d.used)
            sums[part, :] = sums[part, :] + ubuf[k].astype(F32)
        for c in range(d.cl):
            out[c] = sums[pl.ds(c, d.rows, stride=d.cl), :].astype(BF16)

    with phase("gather_wait"):
        for s in range(1, d.levs):
            gather_copy(d, s, total2, gathered, gs, gr, True).wait_recv()
    for k in range(d.levs):
        gflat[k * d.cl : (k + 1) * d.cl, :] = gathered[k]
    for j in range(0, d.channels, W):
        n = min(W, d.channels - j)
        grads[:, j : j + n] = jnp.transpose(gflat[j : j + n, :])[: TAPS * TAPS]
    for s in range(1, d.levs):
        gather_copy(d, s, total2, gathered, gs, gr).wait_send()
    blocks_sent(*residual)
    rows_sent(d, *forward)
    blocks_sent(*upward)
    rows_sent(d, *backward)


def settle(*refs):
    for source, target in zip(refs[:3], refs[3:]):
        target[...] = source[...]


VMEM = pl.BlockSpec(memory_space=pltpu.VMEM)
ANY = pl.BlockSpec(memory_space=pl.ANY)
DMA = pltpu.SemaphoreType.DMA
LIMIT = 60 * 1024 * 1024


def shards(snapshot, cotangent, ocean_mask, kernel, norm_gain, norm_shift, weight_in, weight_out):
    levs, lons = lax.axis_size("lev"), lax.axis_size("lon")
    cl, rows, _ = snapshot.shape
    d = Dims(levs, lons, cl * levs, rows, weight_in.shape[1])
    sds = jax.ShapeDtypeStruct
    f32 = lambda *shape: pltpu.VMEM(shape, F32)
    b16 = lambda *shape: pltpu.VMEM(shape, BF16)
    flat = (d.rows * d.cl, W)
    image = (TAPS, (d.rows + 2 * REACH) * d.cl, W)
    halo = (-(-max(d.packs, REACH) * d.cl // 16) * 16, W)
    north = (-(-REACH * d.cl // 16) * 16, W)
    cells = d.tile * W
    share = (d.cl, W)
    result, d_snapshot, grads = pl.pallas_call(
        functools.partial(block_kernel, d),
        name="block",
        out_shape=(
            sds((d.tile, d.channels, W), BF16), sds((d.cl, d.rows, W), BF16), sds((TAPS * TAPS, d.channels), F32),
        ),
        in_specs=[ANY, VMEM, ANY, VMEM, VMEM, VMEM, ANY, ANY],
        out_specs=(VMEM,) * 3,
        scratch_shapes=[
            f32(*flat), f32(d.quad, d.room, W), f32(W, d.channels), f32(*halo), f32(*image), f32(TAPS * TAPS, d.cl, W),
            f32(*image), f32(TAPS, REACH * d.cl, W), f32(*flat),
            f32(d.channels, W), f32(d.channels, W), f32(d.tile, d.channels, W), f32(d.tile, W),
            b16(cells, d.channels), b16(cells, d.channels), f32(cells, d.channels), f32(d.channels, cells),
            f32(d.levs, d.used, W), b16(*weight_in.shape), b16(*weight_out.shape),
            f32(*share), f32(d.first, *share), f32(*share), f32(d.zhi, *share), f32(*share),
            f32(d.levs, *share), f32(d.channels, W), b16(d.cl, d.rows, W), b16(d.tile, d.channels, W),
            f32(cells, d.hidden), f32(TAPS * TAPS, d.cl, W),
            b16(2 * W, 6 * W), b16(max(d.rows * d.cl // 3, REACH * d.cl), 2 * W), f32(*flat),
            *[b16(*halo), b16(2, *halo), b16(*north), b16(3, *north)] * 2,
            b16(d.levs, d.used, W), b16(d.levs, d.used, W),
            *[b16(d.tile, d.levs, d.room, W)] * 2,
            b16(d.levs, d.used, W), b16(d.levs, d.used, W),
            *[b16(d.tile, d.levs, d.cl, W)] * 2,
            DMA((4,)), *[DMA((5,))] * 4, DMA((d.levs,)), DMA((d.levs,)), DMA((d.tile, d.levs)), DMA((d.tile, d.levs)),
            DMA((d.levs,)), DMA((d.levs,)), DMA((d.tile, d.levs)), DMA((d.tile, d.levs)),
            DMA((d.first,)), DMA((d.first,)), DMA((d.zhi,)), DMA((d.zhi,)), DMA((d.levs,)), DMA((d.levs,)),
        ],
        compiler_params=pltpu.CompilerParams(collective_id=0, has_side_effects=True, vmem_limit_bytes=LIMIT),
    )(
        snapshot, kernel.T, jnp.swapaxes(cotangent, 0, 1), ocean_mask,
        norm_gain.reshape(-1, min(W, d.channels)), norm_shift.reshape(-1, min(W, d.channels)), weight_in, weight_out,
    )
    result, d_snapshot, grads = pl.pallas_call(
        settle,
        name="settle",
        out_shape=tuple(sds(x.shape, x.dtype) for x in (result, d_snapshot, grads)),
        in_specs=[VMEM] * 3,
        out_specs=(VMEM,) * 3,
    )(result, d_snapshot, grads)
    return jnp.swapaxes(result, 0, 1), d_snapshot, grads.T


def solution(mesh):
    placed = (
        P("lev", None, "lon"),
        P(None, "lev", "lon"),
        P("lev", "lon"),
        P(),
        P(),
        P(),
        P(),
        P(),
    )
    return jax.shard_map(
        shards,
        mesh=mesh,
        in_specs=placed,
        out_specs=(P(None, "lev", "lon"), P("lev", None, "lon"), P()),
        check_vma=False,
    )
```
